768 devices in a mesh: rows: 192 (over x, y_lo, z), cols: 4 (over y_hi, core).
Axes of the slice: x: 4, y: 8 (y_hi: 2, y_lo: 4; y = y_hi * 4 + y_lo), z: 12, core: 2. Of those that a mesh axis runs over, the one named last changes fastest.
Arguments:
- row_feat: bfloat16 [3072, 512], P('rows', 'cols'), may hold values from -6 to 6
- col_feat: bfloat16 [4, 192, 512], P('cols', 'rows'), may hold values from -6 to 6
- bucket_ids: int32 [3072, 768], P('rows', 'cols'), may hold values from 0 to 127, as said below
- w_row: bfloat16 [512, 128], replicated, may hold values from -0.25 to 0.25
- w_col: bfloat16 [512, 128], replicated, may hold values from -0.25 to 0.25
- w_out: bfloat16 [128, 128], replicated, may hold values from -0.5 to 0.5
- bias_table: bfloat16 [128, 128], replicated, may hold values from -6 to 6
- kernel_one: bfloat16 [9, 128, 128], replicated, may hold values from -0.1875 to 0.1875
- kernel_two: bfloat16 [9, 128, 128], replicated, may hold values from -0.1875 to 0.1875
Outputs:
- contact: bfloat16 [3072, 768, 128], P('rows', 'cols')
The draws below stay inside these ranges and needn't reach their ends.
Inputs may be any that keep to these rules, and one draw needn't show every extreme that they name: bucket_ids[i, j] = clip(floor((j - i + 3072 + s) * 5 * 128 / (4 (3840))) - 16, 0, 127), where i and j are global bin indices and s is one whole-number offset of the slab along the chromosome, the same for all pairs, with |s| <= 240.
All inputs are finite; a program needn't handle non-finite values.
Results may differ from the reference program's by a relative error of at most 0.015.
Values may be sent and summed in bfloat16 or wider, within the bound.
A program may use at most 32 MiB of HBM per device.

```python
import jax
import jax.numpy as jnp
from jax import lax

FEAT = 512
CH = 128
NB = 128
TR = 16
TC = 192
NR = 3072
NC = 768
COLB = 4


def draw_bucket_ids(key, part):
    total_span = NR + NC
    offset_draw = jax.random.randint(key, (), -(total_span // 16), total_span // 16 + 1, dtype=jnp.int32)
    row_index = jnp.arange(NR, dtype=jnp.int32)[:, None]
    col_index = jnp.arange(NC, dtype=jnp.int32)[None, :]
    bucket_raw = (col_index - row_index + NR + offset_draw) * (5 * NB) // (4 * total_span) - NB // 8
    return jnp.clip(bucket_raw, 0, NB - 1).astype(jnp.int32)


def block_levels(own_key, shape, shards, low, largest):
    factor_of, own = 1.0, jax.random.fold_in(own_key, 6)
    for axis_at, parts in shards:
        steps = jnp.exp(jax.random.uniform(jax.random.fold_in(own, axis_at), (parts,), jnp.float32, low / len(shards), largest / len(shards)))
        factor_of = factor_of * jnp.repeat(steps, shape[axis_at] // parts).reshape([-1 if axis == axis_at else 1 for axis in range(len(shape))])
    return factor_of


def bell_draw(key, shape, deviation, limit, split=(), kind=jnp.bfloat16):
    loudness = block_levels(key, shape, split, -0.22, 0.18) if split else 1.0
    result = jax.random.normal(key, shape, jnp.float32) * deviation * loudness
    return jnp.minimum(jnp.maximum(result, -limit), limit).astype(kind)


def setup_inputs(seed: int = 0) -> dict:
    keys = jax.random.split(jax.random.key(seed), 10)
    return {
        "row_feat": bell_draw(keys[0], (NR, FEAT), 1.0, 6.0, ((0, 192), (1, 4))),
        "col_feat": bell_draw(keys[1], (COLB, TC, FEAT), 1.0, 6.0, ((0, 4), (1, 192))),
        "bucket_ids": draw_bucket_ids(jax.random.fold_in(keys[9], 71), 0),
        "w_row": bell_draw(keys[3], (FEAT, CH), FEAT ** -0.5, 0.25),
        "w_col": bell_draw(keys[4], (FEAT, CH), FEAT ** -0.5, 0.25),
        "w_out": bell_draw(keys[5], (CH, CH), CH ** -0.5, 0.5),
        "bias_table": bell_draw(keys[6], (NB, CH), 1.0, 6.0),
        "kernel_one": bell_draw(keys[7], (9, CH, CH), (9 * CH) ** -0.5, 0.1875),
        "kernel_two": bell_draw(keys[8], (9, CH, CH), (9 * CH) ** -0.5, 0.1875),
    }


def gelu_round(values):
    return jax.nn.gelu(values.astype(jnp.float32)).astype(jnp.bfloat16)


def convolve(source, kernel, dilation):
    height, breadth, channels = source.shape
    padded = jnp.pad(source, ((dilation, dilation), (dilation, dilation), (0, 0)))
    running = jnp.zeros((height * breadth, channels), jnp.float32)
    for row_tap in range(3):
        for col_tap in range(3):
            window = padded[row_tap * dilation:row_tap * dilation + height, col_tap * dilation:col_tap * dilation + breadth]
            running = running + jnp.dot(window.reshape(-1, channels), kernel[3 * row_tap + col_tap], preferred_element_type=jnp.float32)
    return running.reshape(height, breadth, channels)


def reference(row_feat, col_feat, bucket_ids, w_row, w_col, w_out, bias_table, kernel_one, kernel_two):
    row_proj = jnp.dot(row_feat, w_row, preferred_element_type=jnp.float32).astype(jnp.bfloat16)
    col_flat = col_feat.reshape(-1, col_feat.shape[2])
    col_proj = jnp.dot(col_flat, w_col, preferred_element_type=jnp.float32).astype(jnp.bfloat16)
    total_rows = row_proj.shape[0]
    total_cols = col_proj.shape[0]
    channels = row_proj.shape[1]
    buckets = bias_table.shape[0]

    def build(block):
        rows_here, ids_here = block
        outer = (rows_here[:, None, :].astype(jnp.float32) * col_proj[None, :, :].astype(jnp.float32)).astype(jnp.bfloat16)
        onehot = (ids_here.reshape(-1)[:, None] == jnp.arange(buckets, dtype=jnp.int32)[None, :]).astype(jnp.bfloat16)
        mixed = jnp.dot(outer.reshape(-1, channels), w_out, preferred_element_type=jnp.float32)
        mixed = mixed + jnp.dot(onehot, bias_table, preferred_element_type=jnp.float32)
        return mixed.astype(jnp.bfloat16).reshape(rows_here.shape[0], total_cols, channels)

    blocks = total_rows // TR
    pair0 = lax.map(build, (row_proj.reshape(blocks, TR, channels), bucket_ids.reshape(blocks, TR, total_cols)))
    pair0 = pair0.reshape(total_rows, total_cols, channels)
    act0 = gelu_round(pair0)
    pair1 = (pair0.astype(jnp.float32) + convolve(act0, kernel_one, 2)).astype(jnp.bfloat16)
    act1 = gelu_round(pair1)
    return (pair1.astype(jnp.float32) + convolve(act1, kernel_two, 4)).astype(jnp.bfloat16)
```

```python
import functools

import jax
import jax.numpy as jnp
from jax import lax
from jax.experimental import pallas as pl
from jax.experimental.pallas import tpu as pltpu
from jax.sharding import PartitionSpec as P

MESH = pl.DeviceIdType.MESH
F32 = jnp.float32
BF16 = jnp.bfloat16

NX, NY, NZ = 4, 4, 12
NROW, NCOL = NX * NY * NZ, 4
TR, TC, CH = 16, 192, 128
STEP = 24
BASE = 3072
LOW = -240
EXT = 28
WIDE = 208
TAB = 240
CHUNK = 64


def place():
    row, col = lax.axis_index("rows"), lax.axis_index("cols")
    return row, col, row // (NY * NZ), (row // NZ) % NY, row % NZ


def row_at(x, y, z):
    return (x * NY + y) * NZ + z


def send(src, dst, send_sem, recv_sem, device):
    return pltpu.make_async_remote_copy(
        src_ref=src,
        dst_ref=dst,
        send_sem=send_sem,
        recv_sem=recv_sem,
        device_id=device,
        device_id_type=MESH,
    )


def gather_kernel(
    row_feat, col_feat, ids, w_row, w_col,
    cols_out, rows_out, offset_out,
    ybuf, zbuf, flat, xbuf, rbuf, lbuf,
    ysend, yrecv, zsend, zrecv, xsend, xrecv, rsend, rrecv, lsend, lrecv,
):
    row, col, x, y, z = place()
    has_up, has_down = row > 0, row < NROW - 1
    gives_right = (x == NX - 1) & (y == NY - 1) & (col < NCOL - 1)
    gives_left = (x == 0) & (y == 0) & (col > 0)
    takes_left = (x == NX - 1) & (col > 0)
    takes_right = (x == 0) & (col < NCOL - 1)

    ybuf[NY] = jnp.zeros((1, CH), F32)
    flat[NY * NZ + NZ :, :] = jnp.zeros((CHUNK - NY * NZ - NZ, CH), F32)

    @pl.when(jnp.logical_not(has_up))
    def _():
        rbuf[0] = jnp.zeros((NCOL, TR, CH), BF16)
        lbuf[0] = jnp.full((TR, CH), LOW, BF16)

    @pl.when(jnp.logical_not(has_down))
    def _():
        rbuf[2] = jnp.zeros((NCOL, TR, CH), BF16)
        lbuf[2] = jnp.full((TR, CH), LOW, BF16)

    barrier = pltpu.get_barrier_semaphore()

    def greet(device):
        pl.semaphore_signal(barrier, inc=1, device_id=device, device_id_type=MESH)

    for k in range(1, NY):
        greet((row_at(x, (y + k) % NY, z), col))
    for k in range(1, NX):
        greet((row_at((x + k) % NX, y, z), col))
    for k in range(1, NZ):
        greet((row_at(x, y, (z + k) % NZ), col))
    for k in range(1, NCOL):
        greet((row, (col + k) % NCOL))
    expected = NY - 1 + NX - 1 + NZ - 1 + NCOL - 1

    def when_add(cond, amount):
        return jnp.where(cond, amount, 0).astype(jnp.int32)

    @pl.when(has_up)
    def _():
        for k in range(NCOL):
            greet((row - 1, k))

    @pl.when(has_down)
    def _():
        for k in range(NCOL):
            greet((row + 1, k))

    @pl.when(gives_right)
    def _():
        for k in range(NY):
            greet((row_at(x, k, z), col + 1))

    @pl.when(gives_left)
    def _():
        for k in range(NY):
            greet((row_at(x, k, z), col - 1))

    @pl.when(takes_left)
    def _():
        greet((row_at(x, NY - 1, z), col - 1))

    @pl.when(takes_right)
    def _():
        greet((row_at(x, 0, z), col + 1))

    expected = (
        expected
        + when_add(has_up, NCOL)
        + when_add(has_down, NCOL)
        + when_add(gives_right, NY)
        + when_add(gives_left, NY)
        + when_add(takes_left, 1)
        + when_add(takes_right, 1)
    )

    mine = jnp.dot(col_feat[0], w_col[...], preferred_element_type=F32)
    ybuf[y] = mine.astype(BF16).astype(F32)
    rbuf[1, col] = row_feat[...]
    b = ids[...]
    i = lax.broadcasted_iota(jnp.int32, (TR, TC), 0) + row * TR
    j = lax.broadcasted_iota(jnp.int32, (TR, TC), 1) + col * TC
    forced = jnp.where(b >= 1, STEP * (b + 16) - (j - i) - BASE, LOW).astype(F32)
    least = jnp.max(jnp.max(forced, axis=1, keepdims=True), axis=0, keepdims=True)
    least = jnp.maximum(least, float(LOW))
    lbuf[1] = jnp.broadcast_to(least, (TR, CH)).astype(BF16)

    pl.semaphore_wait(barrier, expected)

    ys = []
    for k in range(1, NY):
        to = (y + k) % NY
        copy = send(ybuf.at[y], ybuf.at[y], ysend.at[k], yrecv.at[y], (row_at(x, to, z), col))
        copy.start()
        ys.append(copy)

    def margin_copies(side, to_col, sem):
        return [
            send(ybuf.at[y], ybuf.at[NY], ysend.at[sem + k], yrecv.at[NY], (row_at(x, k, z), to_col))
            for k in range(NY)
        ]

    @pl.when(gives_right)
    def _():
        for copy in margin_copies(0, col + 1, NY):
            copy.start()

    @pl.when(gives_left)
    def _():
        for copy in margin_copies(0, col - 1, 2 * NY):
            copy.start()

    def row_copies(block, to_row, first, skip):
        return [
            send(
                row_feat, rbuf.at[block, col], rsend.at[block, k], rrecv.at[block, col],
                (to_row, (col + k) % NCOL),
            )
            for k in range(skip, NCOL)
        ]

    own = row_copies(1, row, 0, 1)
    for copy in own:
        copy.start()

    def offset_copy(block, to_row):
        return send(lbuf.at[1], lbuf.at[block], lsend.at[block], lrecv.at[block], (to_row, col))

    @pl.when(has_up)
    def _():
        for copy in row_copies(2, row - 1, 0, 0):
            copy.start()
        offset_copy(2, row - 1).start()

    @pl.when(has_down)
    def _():
        for copy in row_copies(0, row + 1, 0, 0):
            copy.start()
        offset_copy(0, row + 1).start()

    def arrived(ref, sem):
        pltpu.make_async_copy(ref, ref, sem).wait()

    for k in range(1, NY):
        at = (y + k) % NY
        arrived(ybuf.at[at], yrecv.at[at])

    @pl.when(takes_left | takes_right)
    def _():
        arrived(ybuf.at[NY], yrecv.at[NY])

    zs = []
    for k in range(1, NZ):
        to = (z + k) % NZ
        copy = send(ybuf, zbuf.at[z], zsend.at[k], zrecv.at[z], (row_at(x, y, to), col))
        copy.start()
        zs.append(copy)
    zbuf[z] = ybuf[...]

    for k in range(1, NCOL):
        at = (col + k) % NCOL
        arrived(rbuf.at[1, at], rrecv.at[1, at])

    @pl.when(has_up)
    def _():
        for k in range(NCOL):
            arrived(rbuf.at[0, k], rrecv.at[0, k])
        arrived(lbuf.at[0], lrecv.at[0])

    @pl.when(has_down)
    def _():
        for k in range(NCOL):
            arrived(rbuf.at[2, k], rrecv.at[2, k])
        arrived(lbuf.at[2], lrecv.at[2])

    sums = jnp.zeros((3 * TR, CH), F32)
    for k in range(NCOL):
        sums = sums + jnp.dot(
            rbuf[:, k].reshape(3 * TR, CH),
            w_row[k * CH : (k + 1) * CH, :],
            preferred_element_type=F32,
        )
    rows_out[...] = sums.astype(BF16).astype(F32)
    offset_out[...] = jnp.maximum(jnp.maximum(lbuf[0], lbuf[1]), lbuf[2]).astype(F32)[0:8]

    for k in range(1, NZ):
        at = (z + k) % NZ
        arrived(zbuf.at[at], zrecv.at[at])

    for a in range(NY + 1):
        for b in range(NZ):
            flat[a * NZ + b : a * NZ + b + 1, :] = zbuf[b, a]
    xbuf[x] = flat[...].astype(BF16)

    xs = []
    for k in range(1, NX):
        to = (x + k) % NX
        copy = send(xbuf.at[x], xbuf.at[x], xsend.at[k], xrecv.at[x], (row_at(to, y, z), col))
        copy.start()
        xs.append(copy)
    for k in range(1, NX):
        at = (x + k) % NX
        arrived(xbuf.at[at], xrecv.at[at])
    cols_out[...] = xbuf[...].reshape(NX * CHUNK, CH)

    for copy in ys + zs + xs + own:
        copy.wait_send()

    @pl.when(gives_right)
    def _():
        for copy in margin_copies(0, col + 1, NY):
            copy.wait_send()

    @pl.when(gives_left)
    def _():
        for copy in margin_copies(0, col - 1, 2 * NY):
            copy.wait_send()

    @pl.when(has_up)
    def _():
        for copy in row_copies(2, row - 1, 0, 0):
            copy.wait_send()
        offset_copy(2, row - 1).wait_send()

    @pl.when(has_down)
    def _():
        for copy in row_copies(0, row + 1, 0, 0):
            copy.wait_send()
        offset_copy(0, row + 1).wait_send()


def gather(row_feat, col_feat, ids, w_row, w_col):
    vmem = pl.BlockSpec(memory_space=pltpu.VMEM)
    dma = pltpu.SemaphoreType.DMA
    return pl.pallas_call(
        gather_kernel,
        out_shape=(
            jax.ShapeDtypeStruct((NX * CHUNK, CH), BF16),
            jax.ShapeDtypeStruct((3 * TR, CH), F32),
            jax.ShapeDtypeStruct((8, CH), F32),
        ),
        in_specs=[vmem] * 5,
        out_specs=(vmem, vmem, vmem),
        scratch_shapes=[
            pltpu.VMEM((NY + 1, 1, CH), F32),
            pltpu.VMEM((NZ, NY + 1, 1, CH), F32),
            pltpu.VMEM((CHUNK, CH), F32),
            pltpu.VMEM((NX, CHUNK, CH), BF16),
            pltpu.VMEM((3, NCOL, TR, CH), BF16),
            pltpu.VMEM((3, TR, CH), BF16),
            dma((3 * NY,)), dma((NY + 1,)),
            dma((NZ,)), dma((NZ,)),
            dma((NX,)), dma((NX,)),
            dma((3, NCOL)), dma((3, NCOL)),
            dma((3,)), dma((3,)),
        ],
        compiler_params=pltpu.CompilerParams(collective_id=0, has_side_effects=True),
    )(row_feat, col_feat, ids, w_row, w_col)


def gelu(value, half):
    inner = value * (0.7978845608028654 + (0.7978845608028654 * 0.044715) * (value * value))
    return (value * half) * (1.0 + jnp.tanh(inner))


def pair_kernel(
    cols_in, rows_in, offset_in, w_out, bias_table, kernel_one, kernel_two,
    out,
    table, colf, shifted, act0, act1, pair0, pair1,
):
    row, col, _, _, _ = place()
    left = jnp.where(col > 0, 1.0, 0.0).astype(F32)
    right = jnp.where(col < NCOL - 1, 1.0, 0.0).astype(F32)

    spot = lax.broadcasted_iota(jnp.int32, (TAB, CH), 0) + (col * TC - row * TR - 2 - (EXT - 1) + BASE)
    bucket = lax.broadcasted_iota(jnp.int32, (TAB, CH), 1)
    at = spot.astype(F32) + offset_in[0:1, :]
    low = jnp.where(bucket == 0, -1e9, (STEP * (bucket + 16)).astype(F32))
    high = jnp.where(bucket == CH - 1, 1e9, (STEP * (bucket + 17)).astype(F32))
    chosen = jnp.where((at >= low) & (at < high), 1.0, 0.0).astype(BF16)
    table[...] = jnp.dot(chosen, bias_table[...], preferred_element_type=F32)

    take = lax.broadcasted_iota(jnp.int32, (WIDE, NX * CHUNK), 0) - 8
    have = lax.broadcasted_iota(jnp.int32, (WIDE, NX * CHUNK), 1)
    block = NY * NZ
    source = (take // block) * CHUNK + take % block
    source = jnp.where(take < 0, (NX - 1) * CHUNK + block + NZ + take, source)
    source = jnp.where(take >= TC, block + take - TC, source)
    order = jnp.where(source == have, 1.0, 0.0).astype(BF16)
    colf[...] = jnp.dot(order, cols_in[...], preferred_element_type=F32)

    shifted[...] = jnp.zeros_like(shifted)

    def inside(bin):
        return jnp.where((bin >= 0) & (bin < TR * NROW), 0.5, 0.0).astype(F32)

    group = 4

    def first(step, carry):
        base = step * group
        outer = [
            (rows_in[pl.ds(TR - 6 + base + k, 1), :] * colf[...]).astype(BF16) for k in range(group)
        ]
        mixed = jnp.dot(
            jnp.concatenate(outer, axis=0), w_out[...], preferred_element_type=F32
        ).reshape(group, WIDE, CH)
        for k in range(group):
            value = (mixed[k] + table[pl.ds(EXT - 1 - base - k, WIDE), :]).astype(BF16)
            pair0[base + k] = value
            act = gelu(value.astype(F32), inside(row * TR - 6 + base + k))
            shifted[k, 8:16, :] = act[0:8] * left
            shifted[k, 16 : WIDE, :] = act[8 : WIDE - 8]
            shifted[k, WIDE : WIDE + 8, :] = act[WIDE - 8 :] * right
        for k in range(group):
            for q in range(3):
                act0[base + k, :, q * CH : (q + 1) * CH] = shifted[
                    k, 8 + 2 * (q - 1) : 8 + 2 * (q - 1) + WIDE, :
                ].astype(BF16)
        return carry

    lax.fori_loop(0, EXT // group, first, 0)

    def second(step, carry):
        base = step * group
        total = jnp.zeros((group * WIDE, CH), F32)
        for p in range(3):
            total = total + jnp.dot(
                act0[pl.ds(base + 2 * p, group)].reshape(group * WIDE, 3 * CH),
                kernel_one[p],
                preferred_element_type=F32,
            )
        total = total.reshape(group, WIDE, CH)
        for k in range(group):
            value = (pair0[base + 2 + k].astype(F32) + total[k]).astype(BF16).astype(F32)
            pair1[base + k] = value[8 : 8 + TC].astype(BF16)
            act = gelu(value, inside(row * TR - 4 + base + k))
            shifted[k, 8:16, :] = act[0:8] * left
            shifted[k, 16 : WIDE, :] = act[8 : WIDE - 8]
            shifted[k, WIDE : WIDE + 8, :] = act[WIDE - 8 :] * right
        for k in range(group):
            for q in range(3):
                act1[base + k, :, q * CH : (q + 1) * CH] = shifted[
                    k, 16 + 4 * (q - 1) : 16 + 4 * (q - 1) + TC, :
                ].astype(BF16)
        return carry

    lax.fori_loop(0, (TR + 8) // group, second, 0)

    def third(step, carry):
        base = step * group
        total = jnp.zeros((group * TC, CH), F32)
        for p in range(3):
            total = total + jnp.dot(
                act1[pl.ds(base + 4 * p, group)].reshape(group * TC, 3 * CH),
                kernel_two[p],
                preferred_element_type=F32,
            )
        total = total.reshape(group, TC, CH)
        for k in range(group):
            out[base + k] = (pair1[base + 4 + k].astype(F32) + total[k]).astype(BF16)
        return carry

    lax.fori_loop(0, TR // group, third, 0)


def pairs(cols, rows, offset, w_out, bias_table, kernel_one, kernel_two):
    vmem = pl.BlockSpec(memory_space=pltpu.VMEM)
    return pl.pallas_call(
        pair_kernel,
        out_shape=jax.ShapeDtypeStruct((TR, TC, CH), BF16),
        in_specs=[vmem] * 7,
        out_specs=vmem,
        scratch_shapes=[
            pltpu.VMEM((TAB, CH), F32),
            pltpu.VMEM((WIDE, CH), F32),
            pltpu.VMEM((4, WIDE + 16, CH), F32),
            pltpu.VMEM((EXT, WIDE, 3 * CH), BF16),
            pltpu.VMEM((TR + 8, TC, 3 * CH), BF16),
            pltpu.VMEM((EXT, WIDE, CH), BF16),
            pltpu.VMEM((TR + 8, TC, CH), BF16),
        ],
        compiler_params=pltpu.CompilerParams(vmem_limit_bytes=48 * 1024 * 1024),
    )(cols, rows, offset, w_out, bias_table, kernel_one.reshape(3, 3 * CH, CH), kernel_two.reshape(3, 3 * CH, CH))


def per_device(
    row_feat, col_feat, bucket_ids, w_row, w_col, w_out, bias_table, kernel_one, kernel_two
):
    cols, rows, offset = gather(row_feat, col_feat, bucket_ids, w_row, w_col)
    return pairs(cols, rows, offset, w_out, bias_table, kernel_one, kernel_two)


def solution(mesh):
    in_specs = (
        P("rows", "cols"),
        P("cols", "rows", None),
        P("rows", "cols"),
        P(),
        P(),
        P(),
        P(),
        P(),
        P(),
    )
    out_specs = P("rows", "cols", None)
    return jax.shard_map(
        per_device, mesh=mesh, in_specs=in_specs, out_specs=out_specs, check_vma=False
    )
```

```python
import functools

import jax
import jax.numpy as jnp
from jax import lax
from jax.experimental import pallas as pl
from jax.experimental.pallas import tpu as pltpu
from jax.sharding import PartitionSpec as P

MESH = pl.DeviceIdType.MESH
F32 = jnp.float32
BF16 = jnp.bfloat16

NX, NY, NZ = 4, 4, 12
NROW, NCOL = NX * NY * NZ, 4
TR, TC, CH = 16, 192, 128
STEP = 24
BASE = 3072
LOW = -240
EXT = 28
WIDE = 208
TAB = 240
CHUNK = 64


def place():
    row, col = lax.axis_index("rows"), lax.axis_index("cols")
    return row, col, row // (NY * NZ), (row // NZ) % NY, row % NZ


def row_at(x, y, z):
    return (x * NY + y) * NZ + z


def send(src, dst, send_sem, recv_sem, device):
    return pltpu.make_async_remote_copy(
        src_ref=src,
        dst_ref=dst,
        send_sem=send_sem,
        recv_sem=recv_sem,
        device_id=device,
        device_id_type=MESH,
    )


def gather_kernel(
    row_feat, col_feat, ids, w_row, w_col, bias_table, w_out_hbm, one_hbm, two_hbm,
    cols_out, rows_out, table, w_out, kernel_one, kernel_two,
    ybuf, zbuf, flat, xbuf, rbuf, lbuf,
    ysend, yrecv, zsend, zrecv, xsend, xrecv, rsend, rrecv, lsend, lrecv, weight_sem,
):
    row, col, x, y, z = place()
    has_up, has_down = row > 0, row < NROW - 1
    gives_right = (x == NX - 1) & (y == NY - 1) & (col < NCOL - 1)
    gives_left = (x == 0) & (y == 0) & (col > 0)
    takes_left = (x == NX - 1) & (col > 0)
    takes_right = (x == 0) & (col < NCOL - 1)

    ybuf[NY] = jnp.zeros((1, CH), F32)
    flat[NY * NZ + NZ :, :] = jnp.zeros((CHUNK - NY * NZ - NZ, CH), F32)

    @pl.when(jnp.logical_not(has_up))
    def _():
        rbuf[0] = jnp.zeros((NCOL, TR, CH), BF16)
        lbuf[0] = jnp.full((TR, CH), LOW, BF16)

    @pl.when(jnp.logical_not(has_down))
    def _():
        rbuf[2] = jnp.zeros((NCOL, TR, CH), BF16)
        lbuf[2] = jnp.full((TR, CH), LOW, BF16)

    barrier = pltpu.get_barrier_semaphore()

    def greet(device):
        pl.semaphore_signal(barrier, inc=1, device_id=device, device_id_type=MESH)

    for k in range(1, NY):
        greet((row_at(x, (y + k) % NY, z), col))
    for k in range(1, NX):
        greet((row_at((x + k) % NX, y, z), col))
    for k in range(1, NZ):
        greet((row_at(x, y, (z + k) % NZ), col))
    for k in range(1, NCOL):
        greet((row, (col + k) % NCOL))
    expected = NY - 1 + NX - 1 + NZ - 1 + NCOL - 1

    def when_add(cond, amount):
        return jnp.where(cond, amount, 0).astype(jnp.int32)

    @pl.when(has_up)
    def _():
        for k in range(NCOL):
            greet((row - 1, k))

    @pl.when(has_down)
    def _():
        for k in range(NCOL):
            greet((row + 1, k))

    @pl.when(gives_right)
    def _():
        for k in range(NY):
            greet((row_at(x, k, z), col + 1))

    @pl.when(gives_left)
    def _():
        for k in range(NY):
            greet((row_at(x, k, z), col - 1))

    @pl.when(takes_left)
    def _():
        greet((row_at(x, NY - 1, z), col - 1))

    @pl.when(takes_right)
    def _():
        greet((row_at(x, 0, z), col + 1))

    expected = (
        expected
        + when_add(has_up, NCOL)
        + when_add(has_down, NCOL)
        + when_add(gives_right, NY)
        + when_add(gives_left, NY)
        + when_add(takes_left, 1)
        + when_add(takes_right, 1)
    )

    weights = [
        pltpu.make_async_copy(src, dst, weight_sem.at[k])
        for k, (src, dst) in enumerate(((w_out_hbm, w_out), (one_hbm, kernel_one), (two_hbm, kernel_two)))
    ]
    for copy in weights:
        copy.start()

    mine = jnp.dot(col_feat[0], w_col[...], preferred_element_type=F32)
    ybuf[y] = mine.astype(BF16).astype(F32)
    rbuf[1, col] = row_feat[...]
    b = ids[...]
    i = lax.broadcasted_iota(jnp.int32, (TR, TC), 0) + row * TR
    j = lax.broadcasted_iota(jnp.int32, (TR, TC), 1) + col * TC
    forced = jnp.where(b >= 1, STEP * (b + 16) - (j - i) - BASE, LOW).astype(F32)
    least = jnp.max(jnp.max(forced, axis=1, keepdims=True), axis=0, keepdims=True)
    least = jnp.maximum(least, float(LOW))
    lbuf[1] = jnp.broadcast_to(least, (TR, CH)).astype(BF16)

    pl.semaphore_wait(barrier, expected)

    ys = []
    for k in range(1, NY):
        to = (y + k) % NY
        copy = send(ybuf.at[y], ybuf.at[y], ysend.at[k], yrecv.at[y], (row_at(x, to, z), col))
        copy.start()
        ys.append(copy)

    def margin_copies(side, to_col, sem):
        return [
            send(ybuf.at[y], ybuf.at[NY], ysend.at[sem + k], yrecv.at[NY], (row_at(x, k, z), to_col))
            for k in range(NY)
        ]

    @pl.when(gives_right)
    def _():
        for copy in margin_copies(0, col + 1, NY):
            copy.start()

    @pl.when(gives_left)
    def _():
        for copy in margin_copies(0, col - 1, 2 * NY):
            copy.start()

    def row_copies(block, to_row, first, skip):
        return [
            send(
                row_feat, rbuf.at[block, col], rsend.at[block, k], rrecv.at[block, col],
                (to_row, (col + k) % NCOL),
            )
            for k in range(skip, NCOL)
        ]

    own = row_copies(1, row, 0, 1)
    for copy in own:
        copy.start()

    def offset_copy(block, to_row):
        return send(lbuf.at[1], lbuf.at[block], lsend.at[block], lrecv.at[block], (to_row, col))

    @pl.when(has_up)
    def _():
        for copy in row_copies(2, row - 1, 0, 0):
            copy.start()
        offset_copy(2, row - 1).start()

    @pl.when(has_down)
    def _():
        for copy in row_copies(0, row + 1, 0, 0):
            copy.start()
        offset_copy(0, row + 1).start()

    def arrived(ref, sem):
        pltpu.make_async_copy(ref, ref, sem).wait()

    for k in range(1, NY):
        at = (y + k) % NY
        arrived(ybuf.at[at], yrecv.at[at])

    @pl.when(takes_left | takes_right)
    def _():
        arrived(ybuf.at[NY], yrecv.at[NY])

    zs = []
    for k in range(1, NZ):
        to = (z + k) % NZ
        copy = send(ybuf, zbuf.at[z], zsend.at[k], zrecv.at[z], (row_at(x, y, to), col))
        copy.start()
        zs.append(copy)
    zbuf[z] = ybuf[...]

    for k in range(1, NCOL):
        at = (col + k) % NCOL
        arrived(rbuf.at[1, at], rrecv.at[1, at])

    @pl.when(has_up)
    def _():
        for k in range(NCOL):
            arrived(rbuf.at[0, k], rrecv.at[0, k])
        arrived(lbuf.at[0], lrecv.at[0])

    @pl.when(has_down)
    def _():
        for k in range(NCOL):
            arrived(rbuf.at[2, k], rrecv.at[2, k])
        arrived(lbuf.at[2], lrecv.at[2])

    sums = jnp.zeros((3 * TR, CH), F32)
    for k in range(NCOL):
        sums = sums + jnp.dot(
            rbuf[:, k].reshape(3 * TR, CH),
            w_row[k * CH : (k + 1) * CH, :],
            preferred_element_type=F32,
        )
    rows_out[...] = sums.astype(BF16).astype(F32)

    offset = jnp.maximum(jnp.maximum(lbuf[0], lbuf[1]), lbuf[2]).astype(F32)
    spot = lax.broadcasted_iota(jnp.int32, (TAB, CH), 0) + (col * TC - row * TR - 2 - (EXT - 1) + BASE)
    bucket = lax.broadcasted_iota(jnp.int32, (TAB, CH), 1)
    at = spot.astype(F32) + offset[0:1, :]
    low = jnp.where(bucket == 0, -1e9, (STEP * (bucket + 16)).astype(F32))
    high = jnp.where(bucket == CH - 1, 1e9, (STEP * (bucket + 17)).astype(F32))
    chosen = jnp.where((at >= low) & (at < high), 1.0, 0.0).astype(BF16)
    table[...] = jnp.dot(chosen, bias_table[...], preferred_element_type=F32)

    for k in range(1, NZ):
        at = (z + k) % NZ
        arrived(zbuf.at[at], zrecv.at[at])

    for a in range(NY + 1):
        for b in range(NZ):
            flat[a * NZ + b : a * NZ + b + 1, :] = zbuf[b, a]
    xbuf[x] = flat[...].astype(BF16)

    xs = []
    for k in range(1, NX):
        to = (x + k) % NX
        copy = send(xbuf.at[x], xbuf.at[x], xsend.at[k], xrecv.at[x], (row_at(to, y, z), col))
        copy.start()
        xs.append(copy)
    for k in range(1, NX):
        at = (x + k) % NX
        arrived(xbuf.at[at], xrecv.at[at])
    cols_out[...] = xbuf[...].reshape(NX * CHUNK, CH)

    for copy in ys + zs + xs + own:
        copy.wait_send()
    for copy in weights:
        copy.wait()

    @pl.when(gives_right)
    def _():
        for copy in margin_copies(0, col + 1, NY):
            copy.wait_send()

    @pl.when(gives_left)
    def _():
        for copy in margin_copies(0, col - 1, 2 * NY):
            copy.wait_send()

    @pl.when(has_up)
    def _():
        for copy in row_copies(2, row - 1, 0, 0):
            copy.wait_send()
        offset_copy(2, row - 1).wait_send()

    @pl.when(has_down)
    def _():
        for copy in row_copies(0, row + 1, 0, 0):
            copy.wait_send()
        offset_copy(0, row + 1).wait_send()


def gather(row_feat, col_feat, ids, w_row, w_col, bias_table, w_out, kernel_one, kernel_two):
    vmem = pl.BlockSpec(memory_space=pltpu.VMEM)
    dma = pltpu.SemaphoreType.DMA
    return pl.pallas_call(
        gather_kernel,
        out_shape=(
            pltpu.VMEM((NX * CHUNK, CH), BF16),
            pltpu.VMEM((3 * TR, CH), F32),
            pltpu.VMEM((TAB, CH), F32),
            pltpu.VMEM((CH, CH), BF16),
            pltpu.VMEM((9, CH, CH), BF16),
            pltpu.VMEM((9, CH, CH), BF16),
        ),
        in_specs=[vmem] * 6 + [pl.BlockSpec(memory_space=pl.ANY)] * 3,
        out_specs=(vmem,) * 6,
        scratch_shapes=[
            pltpu.VMEM((NY + 1, 1, CH), F32),
            pltpu.VMEM((NZ, NY + 1, 1, CH), F32),
            pltpu.VMEM((CHUNK, CH), F32),
            pltpu.VMEM((NX, CHUNK, CH), BF16),
            pltpu.VMEM((3, NCOL, TR, CH), BF16),
            pltpu.VMEM((3, TR, CH), BF16),
            dma((3 * NY,)), dma((NY + 1,)),
            dma((NZ,)), dma((NZ,)),
            dma((NX,)), dma((NX,)),
            dma((3, NCOL)), dma((3, NCOL)),
            dma((3,)), dma((3,)),
            dma((3,)),
        ],
        compiler_params=pltpu.CompilerParams(collective_id=0, has_side_effects=True),
    )(row_feat, col_feat, ids, w_row, w_col, bias_table, w_out, kernel_one, kernel_two)


def gelu(value, half):
    inner = value * (0.7978845608028654 + (0.7978845608028654 * 0.044715) * (value * value))
    return (value * half) * (1.0 + jnp.tanh(inner))


def pair_kernel(
    cols_in, rows_in, table, w_out, kernel_one, kernel_two,
    out,
    colf, shifted, act0, act1, pair0, pair1,
):
    row, col, _, _, _ = place()
    left = jnp.where(col > 0, 1.0, 0.0).astype(F32)
    right = jnp.where(col < NCOL - 1, 1.0, 0.0).astype(F32)

    take = lax.broadcasted_iota(jnp.int32, (WIDE, NX * CHUNK), 0) - 8
    have = lax.broadcasted_iota(jnp.int32, (WIDE, NX * CHUNK), 1)
    block = NY * NZ
    source = (take // block) * CHUNK + take % block
    source = jnp.where(take < 0, (NX - 1) * CHUNK + block + NZ + take, source)
    source = jnp.where(take >= TC, block + take - TC, source)
    order = jnp.where(source == have, 1.0, 0.0).astype(BF16)
    colf[...] = jnp.dot(order, cols_in[...], preferred_element_type=F32)

    shifted[...] = jnp.zeros_like(shifted)

    def inside(bin):
        return jnp.where((bin >= 0) & (bin < TR * NROW), 0.5, 0.0).astype(F32)

    group = 4

    def first(step, carry):
        base = step * group
        outer = [
            (rows_in[pl.ds(TR - 6 + base + k, 1), :] * colf[...]).astype(BF16) for k in range(group)
        ]
        mixed = jnp.dot(
            jnp.concatenate(outer, axis=0), w_out[...], preferred_element_type=F32
        ).reshape(group, WIDE, CH)
        for k in range(group):
            value = (mixed[k] + table[pl.ds(EXT - 1 - base - k, WIDE), :]).astype(BF16)
            pair0[base + k] = value
            act = gelu(value.astype(F32), inside(row * TR - 6 + base + k))
            shifted[k, 8:16, :] = act[0:8] * left
            shifted[k, 16 : WIDE, :] = act[8 : WIDE - 8]
            shifted[k, WIDE : WIDE + 8, :] = act[WIDE - 8 :] * right
        for k in range(group):
            for q in range(3):
                act0[base + k, :, q * CH : (q + 1) * CH] = shifted[
                    k, 8 + 2 * (q - 1) : 8 + 2 * (q - 1) + WIDE, :
                ].astype(BF16)
        return carry

    lax.fori_loop(0, EXT // group, first, 0)

    def second(step, carry):
        base = step * group
        total = jnp.zeros((group * WIDE, CH), F32)
        for p in range(3):
            total = total + jnp.dot(
                act0[pl.ds(base + 2 * p, group)].reshape(group * WIDE, 3 * CH),
                kernel_one[p],
                preferred_element_type=F32,
            )
        total = total.reshape(group, WIDE, CH)
        for k in range(group):
            value = (pair0[base + 2 + k].astype(F32) + total[k]).astype(BF16).astype(F32)
            pair1[base + k] = value[8 : 8 + TC].astype(BF16)
            act = gelu(value, inside(row * TR - 4 + base + k))
            shifted[k, 8:16, :] = act[0:8] * left
            shifted[k, 16 : WIDE, :] = act[8 : WIDE - 8]
            shifted[k, WIDE : WIDE + 8, :] = act[WIDE - 8 :] * right
        for k in range(group):
            for q in range(3):
                act1[base + k, :, q * CH : (q + 1) * CH] = shifted[
                    k, 16 + 4 * (q - 1) : 16 + 4 * (q - 1) + TC, :
                ].astype(BF16)
        return carry

    lax.fori_loop(0, (TR + 8) // group, second, 0)

    def third(step, carry):
        base = step * group
        total = jnp.zeros((group * TC, CH), F32)
        for p in range(3):
            total = total + jnp.dot(
                act1[pl.ds(base + 4 * p, group)].reshape(group * TC, 3 * CH),
                kernel_two[p],
                preferred_element_type=F32,
            )
        total = total.reshape(group, TC, CH)
        for k in range(group):
            out[base + k] = (pair1[base + 4 + k].astype(F32) + total[k]).astype(BF16)
        return carry

    lax.fori_loop(0, TR // group, third, 0)


def pairs(cols, rows, table, w_out, kernel_one, kernel_two):
    vmem = pl.BlockSpec(memory_space=pltpu.VMEM)
    return pl.pallas_call(
        pair_kernel,
        out_shape=jax.ShapeDtypeStruct((TR, TC, CH), BF16),
        in_specs=[vmem] * 6,
        out_specs=vmem,
        scratch_shapes=[
            pltpu.VMEM((WIDE, CH), F32),
            pltpu.VMEM((4, WIDE + 16, CH), F32),
            pltpu.VMEM((EXT, WIDE, 3 * CH), BF16),
            pltpu.VMEM((TR + 8, TC, 3 * CH), BF16),
            pltpu.VMEM((EXT, WIDE, CH), BF16),
            pltpu.VMEM((TR + 8, TC, CH), BF16),
        ],
        compiler_params=pltpu.CompilerParams(vmem_limit_bytes=48 * 1024 * 1024),
    )(cols, rows, table, w_out, kernel_one.reshape(3, 3 * CH, CH), kernel_two.reshape(3, 3 * CH, CH))


def per_device(
    row_feat, col_feat, bucket_ids, w_row, w_col, w_out, bias_table, kernel_one, kernel_two
):
    gathered = gather(
        row_feat, col_feat, bucket_ids, w_row, w_col, bias_table, w_out, kernel_one, kernel_two
    )
    return pairs(*gathered)


def solution(mesh):
    in_specs = (
        P("rows", "cols"),
        P("cols", "rows", None),
        P("rows", "cols"),
        P(),
        P(),
        P(),
        P(),
        P(),
        P(),
    )
    out_specs = P("rows", "cols", None)
    return jax.shard_map(
        per_device, mesh=mesh, in_specs=in_specs, out_specs=out_specs, check_vma=False
    )
```

```python
import functools

import jax
import jax.numpy as jnp
from jax import lax
from jax.experimental import pallas as pl
from jax.experimental.pallas import tpu as pltpu
from jax.sharding import PartitionSpec as P

MESH = pl.DeviceIdType.MESH
F32 = jnp.float32
BF16 = jnp.bfloat16

NX, NY, NZ = 4, 4, 12
NROW, NCOL = NX * NY * NZ, 4
TR, TC, CH = 16, 192, 128
STEP = 24
BASE = 3072
LOW = -240
EXT = 28
WIDE = 208
TAB = 240
CHUNK = 64


def place():
    row, col = lax.axis_index("rows"), lax.axis_index("cols")
    return row, col, row // (NY * NZ), (row // NZ) % NY, row % NZ


def row_at(x, y, z):
    return (x * NY + y) * NZ + z


def send(src, dst, send_sem, recv_sem, device):
    return pltpu.make_async_remote_copy(
        src_ref=src,
        dst_ref=dst,
        send_sem=send_sem,
        recv_sem=recv_sem,
        device_id=device,
        device_id_type=MESH,
    )


SIDE = 6


def gather_kernel(
    row_hbm, col_hbm, ids_hbm, w_row_hbm, w_col_hbm, bias_hbm, w_out_hbm, one_hbm, two_hbm,
    colf, rows_out, table, w_out, kernel_one, kernel_two,
    col_feat, ids, w_row, w_col, bias_table,
    ybuf, zbuf, flat, xbuf, rbuf, pbuf, lbuf,
    load_sem, weight_sem,
    ysend, yrecv, zsend, zrecv, xsend, xrecv, rsend, rrecv, psend, precv, lsend, lrecv,
    below, ready, edge,
):
    row, col, x, y, z = place()
    has_up, has_down = row > 0, row < NROW - 1
    gives_right = (x == NX - 1) & (y == NY - 1) & (col < NCOL - 1)
    gives_left = (x == 0) & (y == 0) & (col > 0)
    takes_left = (x == NX - 1) & (col > 0)
    takes_right = (x == 0) & (col < NCOL - 1)

    loads = [
        pltpu.make_async_copy(src, dst, load_sem.at[k])
        for k, (src, dst) in enumerate((
            (col_hbm, col_feat), (w_col_hbm, w_col), (row_hbm, rbuf.at[col]), (ids_hbm, ids),
            (w_row_hbm, w_row), (bias_hbm, bias_table),
        ))
    ]
    for copy in loads:
        copy.start()

    ybuf[NY] = jnp.zeros((1, CH), F32)

    @pl.when(jnp.logical_not(has_up))
    def _():
        pbuf[0] = jnp.zeros((TR, CH), BF16)
        lbuf[0] = jnp.full((TR, CH), LOW, BF16)

    @pl.when(jnp.logical_not(has_down))
    def _():
        pbuf[2] = jnp.zeros((TR, CH), BF16)
        lbuf[2] = jnp.full((TR, CH), LOW, BF16)

    barrier = pltpu.get_barrier_semaphore()

    def greet(device):
        pl.semaphore_signal(barrier, inc=1, device_id=device, device_id_type=MESH)

    for k in range(1, NY):
        greet((row_at(x, (y + k) % NY, z), col))
    for k in range(1, NCOL):
        greet((row, (col + k) % NCOL))

    @pl.when(z > 0)
    def _():
        greet((row - 1, col))

    @pl.when(z < NZ - 1)
    def _():
        greet((row + 1, col))

    @pl.when((z == 0) & has_up)
    def _():
        greet((row - 1, col))

    @pl.when(gives_right)
    def _():
        for k in range(NY):
            greet((row_at(x, k, z), col + 1))

    @pl.when(gives_left)
    def _():
        for k in range(NY):
            greet((row_at(x, k, z), col - 1))

    @pl.when(takes_left)
    def _():
        greet((row_at(x, NY - 1, z), col - 1))

    @pl.when(takes_right)
    def _():
        greet((row_at(x, 0, z), col + 1))

    for k in range(1, NX):
        greet((row_at((x + k) % NX, y, z), col))

    def when_add(cond, amount):
        return jnp.where(cond, amount, 0).astype(jnp.int32)

    expected = (
        NY - 1 + NX - 1 + NCOL - 1
        + when_add(z > 0, 1)
        + when_add(z < NZ - 1, 1)
        + when_add((z == NZ - 1) & has_down, 1)
        + when_add(gives_right, NY)
        + when_add(gives_left, NY)
        + when_add(takes_left, 1)
        + when_add(takes_right, 1)
    )

    loads[0].wait()
    loads[1].wait()
    mine = jnp.dot(col_feat[0], w_col[...], preferred_element_type=F32)
    ybuf[y] = mine.astype(BF16).astype(F32)
    loads[2].wait()
    loads[3].wait()
    b = ids[...]
    i = lax.broadcasted_iota(jnp.int32, (TR, TC), 0) + row * TR
    j = lax.broadcasted_iota(jnp.int32, (TR, TC), 1) + col * TC
    forced = jnp.where(b >= 1, STEP * (b + 16) - (j - i) - BASE, LOW).astype(F32)
    least = jnp.max(jnp.max(forced, axis=1, keepdims=True), axis=0, keepdims=True)
    least = jnp.maximum(least, float(LOW))
    lbuf[1] = jnp.broadcast_to(least, (TR, CH)).astype(BF16)

    pl.semaphore_wait(barrier, expected)

    ys = []
    for k in range(1, NY):
        to = (y + k) % NY
        copy = send(ybuf.at[y], ybuf.at[y], ysend.at[k], yrecv.at[y], (row_at(x, to, z), col))
        copy.start()
        ys.append(copy)

    def margin_copies(to_col, sem):
        return [
            send(ybuf.at[y], ybuf.at[NY], ysend.at[sem + k], yrecv.at[NY], (row_at(x, k, z), to_col))
            for k in range(NY)
        ]

    @pl.when(gives_right)
    def _():
        for copy in margin_copies(col + 1, NY):
            copy.start()

    @pl.when(gives_left)
    def _():
        for copy in margin_copies(col - 1, 2 * NY):
            copy.start()

    @pl.when(z > 1)
    def _():
        pl.semaphore_wait(below, 1)

    @pl.when((z > 0) & (z < NZ - 1))
    def _():
        pl.semaphore_signal(below, inc=1, device_id=(row + 1, col), device_id_type=MESH)

    for k in range(NZ - 1):
        @pl.when(k < z)
        def _():
            pl.semaphore_signal(
                ready.at[z], inc=1, device_id=(row_at(x, y, k), col), device_id_type=MESH
            )

    @pl.when((z == NZ - 1) & has_down)
    def _():
        pl.semaphore_signal(edge, inc=1, device_id=(row + 1, col), device_id_type=MESH)

    own = [
        send(rbuf.at[col], rbuf.at[col], rsend.at[k], rrecv.at[col], (row, (col + k) % NCOL))
        for k in range(1, NCOL)
    ]
    for copy in own:
        copy.start()

    weights = [
        pltpu.make_async_copy(src, dst, weight_sem.at[k])
        for k, (src, dst) in enumerate(((w_out_hbm, w_out), (one_hbm, kernel_one), (two_hbm, kernel_two)))
    ]
    for copy in weights:
        copy.start()

    def arrived(ref, sem):
        pltpu.make_async_copy(ref, ref, sem).wait()

    for k in range(1, NY):
        at = (y + k) % NY
        arrived(ybuf.at[at], yrecv.at[at])

    @pl.when(takes_left | takes_right)
    def _():
        arrived(ybuf.at[NY], yrecv.at[NY])

    def along(k):
        return send(ybuf, zbuf.at[z], zsend.at[k], zrecv.at[z], (row_at(x, y, k), col))

    for k in range(NZ - 1):
        @pl.when(k < z)
        def _():
            along(k).start()

    zbuf[z] = ybuf[...]
    for k in range(1, NZ):
        @pl.when(k > z)
        def _():
            pl.semaphore_wait(ready.at[k], 1)
            along(k).start()

    loads[4].wait()
    loads[5].wait()
    for k in range(1, NCOL):
        at = (col + k) % NCOL
        arrived(rbuf.at[at], rrecv.at[at])
    sums = jnp.zeros((TR, CH), F32)
    for k in range(NCOL):
        sums = sums + jnp.dot(
            rbuf[k], w_row[k * CH : (k + 1) * CH, :], preferred_element_type=F32
        )
    pbuf[1] = sums.astype(BF16)

    def to_next(block, to_row):
        return [
            send(pbuf.at[1], pbuf.at[block], psend.at[block], precv.at[block], (to_row, col)),
            send(lbuf.at[1], lbuf.at[block], lsend.at[block], lrecv.at[block], (to_row, col)),
        ]

    @pl.when(has_down)
    def _():
        for copy in to_next(0, row + 1):
            copy.start()

    @pl.when(z > 0)
    def _():
        for copy in to_next(2, row - 1):
            copy.start()

    colf[0:8, :] = jnp.zeros((8, CH), F32)
    colf[WIDE - 8 : WIDE, :] = jnp.zeros((8, CH), F32)
    block = NY * NZ
    flat[block + NZ :, :] = jnp.zeros((CHUNK - block - NZ, CH), F32)

    for k in range(1, NZ):
        at = (z + k) % NZ
        arrived(zbuf.at[at], zrecv.at[at])

    for a in range(NY + 1):
        for b in range(NZ):
            flat[a * NZ + b : a * NZ + b + 1, :] = zbuf[b, a]
    xbuf[x] = flat[...].astype(BF16)

    xs = []
    for k in range(1, NX):
        to = (x + k) % NX
        copy = send(xbuf.at[x], xbuf.at[x], xsend.at[k], xrecv.at[x], (row_at(to, y, z), col))
        copy.start()
        xs.append(copy)

    @pl.when((z == 0) & has_up)
    def _():
        pl.semaphore_wait(edge, 1)
        for copy in to_next(2, row - 1):
            copy.start()

    @pl.when(has_up)
    def _():
        arrived(pbuf.at[0], precv.at[0])
        arrived(lbuf.at[0], lrecv.at[0])

    @pl.when(has_down)
    def _():
        arrived(pbuf.at[2], precv.at[2])
        arrived(lbuf.at[2], lrecv.at[2])

    rows_out[...] = pbuf[...].reshape(3 * TR, CH).astype(F32)

    offset = jnp.maximum(jnp.maximum(lbuf[0], lbuf[1]), lbuf[2]).astype(F32)
    spot = lax.broadcasted_iota(jnp.int32, (TAB, CH), 0) + (col * TC - row * TR - 2 - (EXT - 1) + BASE)
    bucket = lax.broadcasted_iota(jnp.int32, (TAB, CH), 1)
    at = spot.astype(F32) + offset[0:1, :]
    low = jnp.where(bucket == 0, -1e9, (STEP * (bucket + 16)).astype(F32))
    high = jnp.where(bucket == CH - 1, 1e9, (STEP * (bucket + 17)).astype(F32))
    chosen = jnp.where((at >= low) & (at < high), 1.0, 0.0).astype(BF16)
    table[...] = jnp.dot(chosen, bias_table[...], preferred_element_type=F32)
    for copy in ys + own:
        copy.wait_send()
    for copy in weights:
        copy.wait()
    for k in range(NZ):
        @pl.when(k != z)
        def _():
            along(k).wait_send()

    @pl.when(gives_right)
    def _():
        for copy in margin_copies(col + 1, NY):
            copy.wait_send()

    @pl.when(gives_left)
    def _():
        for copy in margin_copies(col - 1, 2 * NY):
            copy.wait_send()

    @pl.when(has_up)
    def _():
        for copy in to_next(2, row - 1):
            copy.wait_send()

    @pl.when(has_down)
    def _():
        for copy in to_next(0, row + 1):
            copy.wait_send()

    for k in range(1, NX):
        at = (x + k) % NX
        arrived(xbuf.at[at], xrecv.at[at])
    for k in range(NX):
        part = xbuf[k].astype(F32)
        colf[8 + k * block : 8 + (k + 1) * block, :] = part[0:block]
        if k == 0:
            colf[8 + TC : 8 + TC + SIDE, :] = part[block : block + SIDE]
        if k == NX - 1:
            colf[8 - SIDE : 8, :] = part[block + NZ - SIDE : block + NZ]
    for copy in xs:
        copy.wait_send()


def gather(row_feat, col_feat, ids, w_row, w_col, bias_table, w_out, kernel_one, kernel_two):
    vmem = pl.BlockSpec(memory_space=pltpu.VMEM)
    dma = pltpu.SemaphoreType.DMA
    signal = pltpu.SemaphoreType.REGULAR
    return pl.pallas_call(
        gather_kernel,
        out_shape=(
            pltpu.VMEM((WIDE, CH), F32),
            pltpu.VMEM((3 * TR, CH), F32),
            pltpu.VMEM((TAB, CH), F32),
            pltpu.VMEM((CH, CH), BF16),
            pltpu.VMEM((9, CH, CH), BF16),
            pltpu.VMEM((9, CH, CH), BF16),
        ),
        in_specs=[pl.BlockSpec(memory_space=pl.ANY)] * 9,
        out_specs=(vmem,) * 6,
        scratch_shapes=[
            pltpu.VMEM((1, 1, NCOL * CH), BF16),
            pltpu.VMEM((TR, TC), jnp.int32),
            pltpu.VMEM((NCOL * CH, CH), BF16),
            pltpu.VMEM((NCOL * CH, CH), BF16),
            pltpu.VMEM((CH, CH), BF16),
            pltpu.VMEM((NY + 1, 1, CH), F32),
            pltpu.VMEM((NZ, NY + 1, 1, CH), F32),
            pltpu.VMEM((CHUNK, CH), F32),
            pltpu.VMEM((NX, CHUNK, CH), BF16),
            pltpu.VMEM((NCOL, TR, CH), BF16),
            pltpu.VMEM((3, TR, CH), BF16),
            pltpu.VMEM((3, TR, CH), BF16),
            dma((6,)), dma((3,)),
            dma((3 * NY,)), dma((NY + 1,)),
            dma((NZ,)), dma((NZ,)),
            dma((NX,)), dma((NX,)),
            dma((NCOL,)), dma((NCOL,)),
            dma((3,)), dma((3,)),
            dma((3,)), dma((3,)),
            signal, signal((NZ,)), signal,
        ],
        compiler_params=pltpu.CompilerParams(collective_id=0, has_side_effects=True),
    )(row_feat, col_feat, ids, w_row, w_col, bias_table, w_out, kernel_one, kernel_two)


def gelu(value, half):
    inner = value * (0.7978845608028654 + (0.7978845608028654 * 0.044715) * (value * value))
    return (value * half) * (1.0 + jnp.tanh(inner))


def pair_kernel(
    colf, rows_in, table, w_out, kernel_one, kernel_two,
    out,
    shifted, act0, act1, pair0, pair1,
):
    row, col, _, _, _ = place()
    left = jnp.where(col > 0, 1.0, 0.0).astype(F32)
    right = jnp.where(col < NCOL - 1, 1.0, 0.0).astype(F32)

    shifted[...] = jnp.zeros_like(shifted)

    def inside(bin):
        return jnp.where((bin >= 0) & (bin < TR * NROW), 0.5, 0.0).astype(F32)

    group = 4

    def first(step, carry):
        base = step * group
        outer = [
            (rows_in[pl.ds(TR - 6 + base + k, 1), :] * colf[...]).astype(BF16) for k in range(group)
        ]
        mixed = jnp.dot(
            jnp.concatenate(outer, axis=0), w_out[...], preferred_element_type=F32
        ).reshape(group, WIDE, CH)
        for k in range(group):
            value = (mixed[k] + table[pl.ds(EXT - 1 - base - k, WIDE), :]).astype(BF16)
            pair0[base + k] = value
            act = gelu(value.astype(F32), inside(row * TR - 6 + base + k))
            shifted[k, 8:16, :] = act[0:8] * left
            shifted[k, 16 : WIDE, :] = act[8 : WIDE - 8]
            shifted[k, WIDE : WIDE + 8, :] = act[WIDE - 8 :] * right
        for k in range(group):
            for q in range(3):
                act0[base + k, :, q * CH : (q + 1) * CH] = shifted[
                    k, 8 + 2 * (q - 1) : 8 + 2 * (q - 1) + WIDE, :
                ].astype(BF16)
        return carry

    lax.fori_loop(0, EXT // group, first, 0)

    def second(step, carry):
        base = step * group
        total = jnp.zeros((group * WIDE, CH), F32)
        for p in range(3):
            total = total + jnp.dot(
                act0[pl.ds(base + 2 * p, group)].reshape(group * WIDE, 3 * CH),
                kernel_one[p],
                preferred_element_type=F32,
            )
        total = total.reshape(group, WIDE, CH)
        for k in range(group):
            value = (pair0[base + 2 + k].astype(F32) + total[k]).astype(BF16).astype(F32)
            pair1[base + k] = value[8 : 8 + TC].astype(BF16)
            act = gelu(value, inside(row * TR - 4 + base + k))
            shifted[k, 8:16, :] = act[0:8] * left
            shifted[k, 16 : WIDE, :] = act[8 : WIDE - 8]
            shifted[k, WIDE : WIDE + 8, :] = act[WIDE - 8 :] * right
        for k in range(group):
            for q in range(3):
                act1[base + k, :, q * CH : (q + 1) * CH] = shifted[
                    k, 16 + 4 * (q - 1) : 16 + 4 * (q - 1) + TC, :
                ].astype(BF16)
        return carry

    lax.fori_loop(0, (TR + 8) // group, second, 0)

    def third(step, carry):
        base = step * group
        total = jnp.zeros((group * TC, CH), F32)
        for p in range(3):
            total = total + jnp.dot(
                act1[pl.ds(base + 4 * p, group)].reshape(group * TC, 3 * CH),
                kernel_two[p],
                preferred_element_type=F32,
            )
        total = total.reshape(group, TC, CH)
        for k in range(group):
            out[base + k] = (pair1[base + 4 + k].astype(F32) + total[k]).astype(BF16)
        return carry

    lax.fori_loop(0, TR // group, third, 0)


def pairs(cols, rows, table, w_out, kernel_one, kernel_two):
    vmem = pl.BlockSpec(memory_space=pltpu.VMEM)
    return pl.pallas_call(
        pair_kernel,
        out_shape=jax.ShapeDtypeStruct((TR, TC, CH), BF16),
        in_specs=[vmem] * 6,
        out_specs=vmem,
        scratch_shapes=[
            pltpu.VMEM((4, WIDE + 16, CH), F32),
            pltpu.VMEM((EXT, WIDE, 3 * CH), BF16),
            pltpu.VMEM((TR + 8, TC, 3 * CH), BF16),
            pltpu.VMEM((EXT, WIDE, CH), BF16),
            pltpu.VMEM((TR + 8, TC, CH), BF16),
        ],
        compiler_params=pltpu.CompilerParams(vmem_limit_bytes=48 * 1024 * 1024),
    )(cols, rows, table, w_out, kernel_one.reshape(3, 3 * CH, CH), kernel_two.reshape(3, 3 * CH, CH))


def per_device(
    row_feat, col_feat, bucket_ids, w_row, w_col, w_out, bias_table, kernel_one, kernel_two
):
    gathered = gather(
        row_feat, col_feat, bucket_ids, w_row, w_col, bias_table, w_out, kernel_one, kernel_two
    )
    return pairs(*gathered)


def solution(mesh):
    in_specs = (
        P("rows", "cols"),
        P("cols", "rows", None),
        P("rows", "cols"),
        P(),
        P(),
        P(),
        P(),
        P(),
        P(),
    )
    out_specs = P("rows", "cols", None)
    return jax.shard_map(
        per_device, mesh=mesh, in_specs=in_specs, out_specs=out_specs, check_vma=False
    )
```

```python
import functools

import jax
import jax.numpy as jnp
from jax import lax
from jax.experimental import pallas as pl
from jax.experimental.pallas import tpu as pltpu
from jax.sharding import PartitionSpec as P

MESH = pl.DeviceIdType.MESH
F32 = jnp.float32
BF16 = jnp.bfloat16

NX, NY, NZ = 4, 4, 12
NROW, NCOL = NX * NY * NZ, 4
TR, TC, CH = 16, 192, 128
STEP = 24
BASE = 3072
LOW = -240
EXT = 28
WIDE = 208
TAB = 240
CHUNK = 64


def place():
    row, col = lax.axis_index("rows"), lax.axis_index("cols")
    return row, col, row // (NY * NZ), (row // NZ) % NY, row % NZ


def row_at(x, y, z):
    return (x * NY + y) * NZ + z


def send(src, dst, send_sem, recv_sem, device):
    return pltpu.make_async_remote_copy(
        src_ref=src,
        dst_ref=dst,
        send_sem=send_sem,
        recv_sem=recv_sem,
        device_id=device,
        device_id_type=MESH,
    )


SIDE = 6


def gather_kernel(
    row_hbm, col_hbm, ids_hbm, w_row_hbm, w_col_hbm, bias_hbm, w_out_hbm, one_hbm, two_hbm,
    colf, rows_out, table, w_out, kernel_one, kernel_two,
    col_feat, ids, w_row, w_col, bias_table,
    ybuf, zbuf, flat, xbuf, rbuf, pbuf, lbuf,
    load_sem, weight_sem,
    ysend, yrecv, zsend, zrecv, xsend, xrecv, rsend, rrecv, psend, precv, lsend, lrecv,
    below, ready, edge,
):
    row, col, x, y, z = place()
    has_up, has_down = row > 0, row < NROW - 1
    gives_right = (x == NX - 1) & (y == NY - 1) & (col < NCOL - 1)
    gives_left = (x == 0) & (y == 0) & (col > 0)
    takes_left = (x == NX - 1) & (col > 0)
    takes_right = (x == 0) & (col < NCOL - 1)

    loads = [
        pltpu.make_async_copy(src, dst, load_sem.at[k])
        for k, (src, dst) in enumerate((
            (col_hbm, col_feat), (w_col_hbm, w_col), (row_hbm, rbuf.at[col]), (ids_hbm, ids),
            (w_row_hbm, w_row), (bias_hbm, bias_table),
        ))
    ]
    for copy in loads:
        copy.start()

    ybuf[NY] = jnp.zeros((1, CH), F32)

    @pl.when(jnp.logical_not(has_up))
    def _():
        pbuf[0] = jnp.zeros((TR, CH), BF16)
        lbuf[0] = jnp.full((TR, CH), LOW, BF16)

    @pl.when(jnp.logical_not(has_down))
    def _():
        pbuf[2] = jnp.zeros((TR, CH), BF16)
        lbuf[2] = jnp.full((TR, CH), LOW, BF16)

    barrier = pltpu.get_barrier_semaphore()

    def greet(device):
        pl.semaphore_signal(barrier, inc=1, device_id=device, device_id_type=MESH)

    for k in range(1, NY):
        greet((row_at(x, (y + k) % NY, z), col))
    for k in range(1, NCOL):
        greet((row, (col + k) % NCOL))

    @pl.when(z > 0)
    def _():
        greet((row - 1, col))

    @pl.when(z < NZ - 1)
    def _():
        greet((row + 1, col))

    @pl.when((z == 0) & has_up)
    def _():
        greet((row - 1, col))

    @pl.when(gives_right)
    def _():
        for k in range(NY):
            greet((row_at(x, k, z), col + 1))

    @pl.when(gives_left)
    def _():
        for k in range(NY):
            greet((row_at(x, k, z), col - 1))

    @pl.when(takes_left)
    def _():
        greet((row_at(x, NY - 1, z), col - 1))

    @pl.when(takes_right)
    def _():
        greet((row_at(x, 0, z), col + 1))

    for k in range(1, NX):
        greet((row_at((x + k) % NX, y, z), col))

    def when_add(cond, amount):
        return jnp.where(cond, amount, 0).astype(jnp.int32)

    expected = (
        NY - 1 + NX - 1 + NCOL - 1
        + when_add(z > 0, 1)
        + when_add(z < NZ - 1, 1)
        + when_add((z == NZ - 1) & has_down, 1)
        + when_add(gives_right, NY)
        + when_add(gives_left, NY)
        + when_add(takes_left, 1)
        + when_add(takes_right, 1)
    )

    loads[0].wait()
    loads[1].wait()
    mine = jnp.dot(col_feat[0], w_col[...], preferred_element_type=F32)
    ybuf[y] = mine.astype(BF16).astype(F32)
    loads[2].wait()
    loads[3].wait()
    b = ids[...]
    i = lax.broadcasted_iota(jnp.int32, (TR, TC), 0) + row * TR
    j = lax.broadcasted_iota(jnp.int32, (TR, TC), 1) + col * TC
    forced = jnp.where(b >= 1, STEP * (b + 16) - (j - i) - BASE, LOW).astype(F32)
    least = jnp.max(jnp.max(forced, axis=1, keepdims=True), axis=0, keepdims=True)
    least = jnp.maximum(least, float(LOW))
    lbuf[1] = jnp.broadcast_to(least, (TR, CH)).astype(BF16)

    pl.semaphore_wait(barrier, expected)

    ys = []
    for k in range(1, NY):
        to = (y + k) % NY
        copy = send(ybuf.at[y], ybuf.at[y], ysend.at[k], yrecv.at[y], (row_at(x, to, z), col))
        copy.start()
        ys.append(copy)

    def margin_copies(to_col, sem):
        return [
            send(ybuf.at[y], ybuf.at[NY], ysend.at[sem + k], yrecv.at[NY], (row_at(x, k, z), to_col))
            for k in range(NY)
        ]

    @pl.when(gives_right)
    def _():
        for copy in margin_copies(col + 1, NY):
            copy.start()

    @pl.when(gives_left)
    def _():
        for copy in margin_copies(col - 1, 2 * NY):
            copy.start()

    @pl.when(z > 1)
    def _():
        pl.semaphore_wait(below, 1)

    @pl.when((z > 0) & (z < NZ - 1))
    def _():
        pl.semaphore_signal(below, inc=1, device_id=(row + 1, col), device_id_type=MESH)

    for k in range(NZ - 1):
        @pl.when(k < z)
        def _():
            pl.semaphore_signal(
                ready.at[z], inc=1, device_id=(row_at(x, y, k), col), device_id_type=MESH
            )

    @pl.when((z == NZ - 1) & has_down)
    def _():
        pl.semaphore_signal(edge, inc=1, device_id=(row + 1, col), device_id_type=MESH)

    own = [
        send(rbuf.at[col], rbuf.at[col], rsend.at[k], rrecv.at[col], (row, (col + k) % NCOL))
        for k in range(1, NCOL)
    ]
    for copy in own:
        copy.start()

    weights = [
        pltpu.make_async_copy(src, dst, weight_sem.at[k])
        for k, (src, dst) in enumerate(((w_out_hbm, w_out), (one_hbm, kernel_one), (two_hbm, kernel_two)))
    ]
    for copy in weights:
        copy.start()

    def arrived(ref, sem):
        pltpu.make_async_copy(ref, ref, sem).wait()

    for k in range(1, NY):
        at = (y + k) % NY
        arrived(ybuf.at[at], yrecv.at[at])

    @pl.when(takes_left | takes_right)
    def _():
        arrived(ybuf.at[NY], yrecv.at[NY])

    def along(k):
        return send(ybuf, zbuf.at[z], zsend.at[k], zrecv.at[z], (row_at(x, y, k), col))

    for k in range(NZ - 1):
        @pl.when(k < z)
        def _():
            along(k).start()

    zbuf[z] = ybuf[...]
    for k in range(1, NZ):
        @pl.when(k > z)
        def _():
            pl.semaphore_wait(ready.at[k], 1)
            along(k).start()

    loads[4].wait()
    loads[5].wait()
    for k in range(1, NCOL):
        at = (col + k) % NCOL
        arrived(rbuf.at[at], rrecv.at[at])
    sums = jnp.zeros((TR, CH), F32)
    for k in range(NCOL):
        sums = sums + jnp.dot(
            rbuf[k], w_row[k * CH : (k + 1) * CH, :], preferred_element_type=F32
        )
    pbuf[1] = sums.astype(BF16)

    def to_next(block, to_row):
        return [
            send(pbuf.at[1], pbuf.at[block], psend.at[block], precv.at[block], (to_row, col)),
            send(lbuf.at[1], lbuf.at[block], lsend.at[block], lrecv.at[block], (to_row, col)),
        ]

    @pl.when(has_down)
    def _():
        for copy in to_next(0, row + 1):
            copy.start()

    @pl.when(z > 0)
    def _():
        for copy in to_next(2, row - 1):
            copy.start()

    colf[0:8, :] = jnp.zeros((8, CH), F32)
    colf[WIDE - 8 : WIDE, :] = jnp.zeros((8, CH), F32)
    block = NY * NZ
    flat[block + NZ :, :] = jnp.zeros((CHUNK - block - NZ, CH), F32)

    for k in range(1, NZ):
        at = (z + k) % NZ
        arrived(zbuf.at[at], zrecv.at[at])

    for a in range(NY + 1):
        for b in range(NZ):
            flat[a * NZ + b : a * NZ + b + 1, :] = zbuf[b, a]
    xbuf[x] = flat[...].astype(BF16)

    xs = []
    for k in range(1, NX):
        to = (x + k) % NX
        copy = send(xbuf.at[x], xbuf.at[x], xsend.at[k], xrecv.at[x], (row_at(to, y, z), col))
        copy.start()
        xs.append(copy)

    @pl.when((z == 0) & has_up)
    def _():
        pl.semaphore_wait(edge, 1)
        for copy in to_next(2, row - 1):
            copy.start()

    @pl.when(has_up)
    def _():
        arrived(pbuf.at[0], precv.at[0])
        arrived(lbuf.at[0], lrecv.at[0])

    @pl.when(has_down)
    def _():
        arrived(pbuf.at[2], precv.at[2])
        arrived(lbuf.at[2], lrecv.at[2])

    rows_out[...] = pbuf[...].reshape(3 * TR, CH).astype(F32)

    offset = jnp.maximum(jnp.maximum(lbuf[0], lbuf[1]), lbuf[2]).astype(F32)
    spot = lax.broadcasted_iota(jnp.int32, (TAB, CH), 0) + (col * TC - row * TR - 2 - (EXT - 1) + BASE)
    bucket = lax.broadcasted_iota(jnp.int32, (TAB, CH), 1)
    at = spot.astype(F32) + offset[0:1, :]
    low = jnp.where(bucket == 0, -1e9, (STEP * (bucket + 16)).astype(F32))
    high = jnp.where(bucket == CH - 1, 1e9, (STEP * (bucket + 17)).astype(F32))
    chosen = jnp.where((at >= low) & (at < high), 1.0, 0.0).astype(BF16)
    table[...] = jnp.dot(chosen, bias_table[...], preferred_element_type=F32)
    for copy in ys + own:
        copy.wait_send()
    for copy in weights:
        copy.wait()
    for k in range(NZ):
        @pl.when(k != z)
        def _():
            along(k).wait_send()

    @pl.when(gives_right)
    def _():
        for copy in margin_copies(col + 1, NY):
            copy.wait_send()

    @pl.when(gives_left)
    def _():
        for copy in margin_copies(col - 1, 2 * NY):
            copy.wait_send()

    @pl.when(has_up)
    def _():
        for copy in to_next(2, row - 1):
            copy.wait_send()

    @pl.when(has_down)
    def _():
        for copy in to_next(0, row + 1):
            copy.wait_send()

    for k in range(1, NX):
        at = (x + k) % NX
        arrived(xbuf.at[at], xrecv.at[at])
    for k in range(NX):
        part = xbuf[k].astype(F32)
        colf[8 + k * block : 8 + (k + 1) * block, :] = part[0:block]
        if k == 0:
            colf[8 + TC : 8 + TC + SIDE, :] = part[block : block + SIDE]
        if k == NX - 1:
            colf[8 - SIDE : 8, :] = part[block + NZ - SIDE : block + NZ]
    for copy in xs:
        copy.wait_send()


def gather(row_feat, col_feat, ids, w_row, w_col, bias_table, w_out, kernel_one, kernel_two):
    vmem = pl.BlockSpec(memory_space=pltpu.VMEM)
    dma = pltpu.SemaphoreType.DMA
    signal = pltpu.SemaphoreType.REGULAR
    return pl.pallas_call(
        gather_kernel,
        out_shape=(
            pltpu.VMEM((WIDE, CH), F32),
            pltpu.VMEM((3 * TR, CH), F32),
            pltpu.VMEM((TAB, CH), F32),
            pltpu.VMEM((CH, CH), BF16),
            pltpu.VMEM((9, CH, CH), BF16),
            pltpu.VMEM((9, CH, CH), BF16),
        ),
        in_specs=[pl.BlockSpec(memory_space=pl.ANY)] * 9,
        out_specs=(vmem,) * 6,
        scratch_shapes=[
            pltpu.VMEM((1, 1, NCOL * CH), BF16),
            pltpu.VMEM((TR, TC), jnp.int32),
            pltpu.VMEM((NCOL * CH, CH), BF16),
            pltpu.VMEM((NCOL * CH, CH), BF16),
            pltpu.VMEM((CH, CH), BF16),
            pltpu.VMEM((NY + 1, 1, CH), F32),
            pltpu.VMEM((NZ, NY + 1, 1, CH), F32),
            pltpu.VMEM((CHUNK, CH), F32),
            pltpu.VMEM((NX, CHUNK, CH), BF16),
            pltpu.VMEM((NCOL, TR, CH), BF16),
            pltpu.VMEM((3, TR, CH), BF16),
            pltpu.VMEM((3, TR, CH), BF16),
            dma((6,)), dma((3,)),
            dma((3 * NY,)), dma((NY + 1,)),
            dma((NZ,)), dma((NZ,)),
            dma((NX,)), dma((NX,)),
            dma((NCOL,)), dma((NCOL,)),
            dma((3,)), dma((3,)),
            dma((3,)), dma((3,)),
            signal, signal((NZ,)), signal,
        ],
        compiler_params=pltpu.CompilerParams(collective_id=0, has_side_effects=True),
    )(row_feat, col_feat, ids, w_row, w_col, bias_table, w_out, kernel_one, kernel_two)


def gelu(value, half):
    inner = value * (0.7978845608028654 + (0.7978845608028654 * 0.044715) * (value * value))
    return (value * half) * (1.0 + jnp.tanh(inner))


def pair_kernel(
    colf, rows_in, table, w_out, kernel_one, kernel_two,
    out,
    shifted, act0, act1, pair0, pair1,
):
    row, col, _, _, _ = place()
    left = jnp.where(col > 0, 1.0, 0.0).astype(F32)
    right = jnp.where(col < NCOL - 1, 1.0, 0.0).astype(F32)

    shifted[...] = jnp.zeros_like(shifted)

    def inside(bin):
        return jnp.where((bin >= 0) & (bin < TR * NROW), 0.5, 0.0).astype(F32)

    group = 4

    def first(step, carry):
        base = step * group
        outer = [
            (rows_in[pl.ds(TR - 6 + base + k, 1), :] * colf[...]).astype(BF16) for k in range(group)
        ]
        mixed = jnp.dot(
            jnp.concatenate(outer, axis=0), w_out[...], preferred_element_type=F32
        ).reshape(group, WIDE, CH)
        for k in range(group):
            value = (mixed[k] + table[pl.ds(EXT - 1 - base - k, WIDE), :]).astype(BF16)
            pair0[base + k] = value
            act = gelu(value.astype(F32), inside(row * TR - 6 + base + k))
            shifted[k, 8:16, :] = act[0:8] * left
            shifted[k, 16 : WIDE, :] = act[8 : WIDE - 8]
            shifted[k, WIDE : WIDE + 8, :] = act[WIDE - 8 :] * right
        for k in range(group):
            for q in range(3):
                act0[base + k, :, q * CH : (q + 1) * CH] = shifted[
                    k, 8 + 2 * (q - 1) : 8 + 2 * (q - 1) + WIDE, :
                ].astype(BF16)
        return carry

    lax.fori_loop(0, EXT // group, first, 0)

    def second(step, carry):
        base = step * group
        total = jnp.dot(
            jnp.concatenate(
                [act0[pl.ds(base + 2 * p, group)].reshape(group * WIDE, 3 * CH) for p in range(3)],
                axis=1,
            ),
            kernel_one[...].reshape(9 * CH, CH),
            preferred_element_type=F32,
        )
        total = total.reshape(group, WIDE, CH)
        for k in range(group):
            value = (pair0[base + 2 + k].astype(F32) + total[k]).astype(BF16).astype(F32)
            pair1[base + k] = value[8 : 8 + TC].astype(BF16)
            act = gelu(value, inside(row * TR - 4 + base + k))
            shifted[k, 8:16, :] = act[0:8] * left
            shifted[k, 16 : WIDE, :] = act[8 : WIDE - 8]
            shifted[k, WIDE : WIDE + 8, :] = act[WIDE - 8 :] * right
        for k in range(group):
            for q in range(3):
                act1[base + k, :, q * CH : (q + 1) * CH] = shifted[
                    k, 16 + 4 * (q - 1) : 16 + 4 * (q - 1) + TC, :
                ].astype(BF16)
        return carry

    lax.fori_loop(0, (TR + 8) // group, second, 0)

    def third(step, carry):
        base = step * group
        total = jnp.dot(
            jnp.concatenate(
                [act1[pl.ds(base + 4 * p, group)].reshape(group * TC, 3 * CH) for p in range(3)],
                axis=1,
            ),
            kernel_two[...].reshape(9 * CH, CH),
            preferred_element_type=F32,
        )
        total = total.reshape(group, TC, CH)
        for k in range(group):
            out[base + k] = (pair1[base + 4 + k].astype(F32) + total[k]).astype(BF16)
        return carry

    lax.fori_loop(0, TR // group, third, 0)


def pairs(cols, rows, table, w_out, kernel_one, kernel_two):
    vmem = pl.BlockSpec(memory_space=pltpu.VMEM)
    return pl.pallas_call(
        pair_kernel,
        out_shape=jax.ShapeDtypeStruct((TR, TC, CH), BF16),
        in_specs=[vmem] * 6,
        out_specs=vmem,
        scratch_shapes=[
            pltpu.VMEM((4, WIDE + 16, CH), F32),
            pltpu.VMEM((EXT, WIDE, 3 * CH), BF16),
            pltpu.VMEM((TR + 8, TC, 3 * CH), BF16),
            pltpu.VMEM((EXT, WIDE, CH), BF16),
            pltpu.VMEM((TR + 8, TC, CH), BF16),
        ],
        compiler_params=pltpu.CompilerParams(vmem_limit_bytes=48 * 1024 * 1024),
    )(cols, rows, table, w_out, kernel_one.reshape(3, 3 * CH, CH), kernel_two.reshape(3, 3 * CH, CH))


def per_device(
    row_feat, col_feat, bucket_ids, w_row, w_col, w_out, bias_table, kernel_one, kernel_two
):
    gathered = gather(
        row_feat, col_feat, bucket_ids, w_row, w_col, bias_table, w_out, kernel_one, kernel_two
    )
    return pairs(*gathered)


def solution(mesh):
    in_specs = (
        P("rows", "cols"),
        P("cols", "rows", None),
        P("rows", "cols"),
        P(),
        P(),
        P(),
        P(),
        P(),
        P(),
    )
    out_specs = P("rows", "cols", None)
    return jax.shard_map(
        per_device, mesh=mesh, in_specs=in_specs, out_specs=out_specs, check_vma=False
    )
```

```python
import functools

import jax
import jax.numpy as jnp
from jax import lax
from jax.experimental import pallas as pl
from jax.experimental.pallas import tpu as pltpu
from jax.sharding import PartitionSpec as P

MESH = pl.DeviceIdType.MESH
F32 = jnp.float32
BF16 = jnp.bfloat16

NX, NY, NZ = 4, 4, 12
NROW, NCOL = NX * NY * NZ, 4
TR, TC, CH = 16, 192, 128
STEP = 24
GROUP = 4
BASE = 3072
LOW = -240
EXT = 28
WIDE = 208
TAB = 240
CHUNK = 64


def place():
    row, col = lax.axis_index("rows"), lax.axis_index("cols")
    return row, col, row // (NY * NZ), (row // NZ) % NY, row % NZ


def row_at(x, y, z):
    return (x * NY + y) * NZ + z


def send(src, dst, send_sem, recv_sem, device):
    return pltpu.make_async_remote_copy(
        src_ref=src,
        dst_ref=dst,
        send_sem=send_sem,
        recv_sem=recv_sem,
        device_id=device,
        device_id_type=MESH,
    )


SIDE = 6


def gather_kernel(
    row_hbm, col_hbm, ids_hbm, w_row_hbm, w_col_hbm, bias_hbm, w_out_hbm, one_hbm, two_hbm,
    colf, rows_out, table, w_out, one_wide, one_narrow, two_wide, two_narrow,
    col_feat, ids, w_row, w_col, bias_table,
    ybuf, zbuf, flat, xbuf, rbuf, pbuf, lbuf,
    load_sem, weight_sem,
    ysend, yrecv, zsend, zrecv, xsend, xrecv, rsend, rrecv, psend, precv, lsend, lrecv,
    below, ready, edge,
):
    row, col, x, y, z = place()
    has_up, has_down = row > 0, row < NROW - 1
    gives_right = (x == NX - 1) & (y == NY - 1) & (col < NCOL - 1)
    gives_left = (x == 0) & (y == 0) & (col > 0)
    takes_left = (x == NX - 1) & (col > 0)
    takes_right = (x == 0) & (col < NCOL - 1)

    loads = [
        pltpu.make_async_copy(src, dst, load_sem.at[k])
        for k, (src, dst) in enumerate((
            (col_hbm, col_feat), (w_col_hbm, w_col), (row_hbm, rbuf.at[col]), (ids_hbm, ids),
            (w_row_hbm, w_row), (bias_hbm, bias_table),
        ))
    ]
    for copy in loads:
        copy.start()

    ybuf[NY] = jnp.zeros((1, CH), F32)

    @pl.when(jnp.logical_not(has_up))
    def _():
        pbuf[0] = jnp.zeros((TR, CH), BF16)
        lbuf[0] = jnp.full((TR, CH), LOW, BF16)

    @pl.when(jnp.logical_not(has_down))
    def _():
        pbuf[2] = jnp.zeros((TR, CH), BF16)
        lbuf[2] = jnp.full((TR, CH), LOW, BF16)

    barrier = pltpu.get_barrier_semaphore()

    def greet(device):
        pl.semaphore_signal(barrier, inc=1, device_id=device, device_id_type=MESH)

    for k in range(1, NY):
        greet((row_at(x, (y + k) % NY, z), col))
    for k in range(1, NCOL):
        greet((row, (col + k) % NCOL))

    @pl.when(z > 0)
    def _():
        greet((row - 1, col))

    @pl.when(z < NZ - 1)
    def _():
        greet((row + 1, col))

    @pl.when((z == 0) & has_up)
    def _():
        greet((row - 1, col))

    @pl.when(gives_right)
    def _():
        for k in range(NY):
            greet((row_at(x, k, z), col + 1))

    @pl.when(gives_left)
    def _():
        for k in range(NY):
            greet((row_at(x, k, z), col - 1))

    @pl.when(takes_left)
    def _():
        greet((row_at(x, NY - 1, z), col - 1))

    @pl.when(takes_right)
    def _():
        greet((row_at(x, 0, z), col + 1))

    for k in range(1, NX):
        greet((row_at((x + k) % NX, y, z), col))

    def when_add(cond, amount):
        return jnp.where(cond, amount, 0).astype(jnp.int32)

    expected = (
        NY - 1 + NX - 1 + NCOL - 1
        + when_add(z > 0, 1)
        + when_add(z < NZ - 1, 1)
        + when_add((z == NZ - 1) & has_down, 1)
        + when_add(gives_right, NY)
        + when_add(gives_left, NY)
        + when_add(takes_left, 1)
        + when_add(takes_right, 1)
    )

    loads[0].wait()
    loads[1].wait()
    mine = jnp.dot(col_feat[0], w_col[...], preferred_element_type=F32)
    ybuf[y] = mine.astype(BF16).astype(F32)
    loads[2].wait()
    loads[3].wait()
    b = ids[...]
    i = lax.broadcasted_iota(jnp.int32, (TR, TC), 0) + row * TR
    j = lax.broadcasted_iota(jnp.int32, (TR, TC), 1) + col * TC
    forced = jnp.where(b >= 1, STEP * (b + 16) - (j - i) - BASE, LOW).astype(F32)
    least = jnp.max(jnp.max(forced, axis=1, keepdims=True), axis=0, keepdims=True)
    least = jnp.maximum(least, float(LOW))
    lbuf[1] = jnp.broadcast_to(least, (TR, CH)).astype(BF16)

    pl.semaphore_wait(barrier, expected)

    ys = []
    for k in range(1, NY):
        to = (y + k) % NY
        copy = send(ybuf.at[y], ybuf.at[y], ysend.at[k], yrecv.at[y], (row_at(x, to, z), col))
        copy.start()
        ys.append(copy)

    def margin_copies(to_col, sem):
        return [
            send(ybuf.at[y], ybuf.at[NY], ysend.at[sem + k], yrecv.at[NY], (row_at(x, k, z), to_col))
            for k in range(NY)
        ]

    @pl.when(gives_right)
    def _():
        for copy in margin_copies(col + 1, NY):
            copy.start()

    @pl.when(gives_left)
    def _():
        for copy in margin_copies(col - 1, 2 * NY):
            copy.start()

    @pl.when(z > 1)
    def _():
        pl.semaphore_wait(below, 1)

    @pl.when((z > 0) & (z < NZ - 1))
    def _():
        pl.semaphore_signal(below, inc=1, device_id=(row + 1, col), device_id_type=MESH)

    for k in range(NZ - 1):
        @pl.when(k < z)
        def _():
            pl.semaphore_signal(
                ready.at[z], inc=1, device_id=(row_at(x, y, k), col), device_id_type=MESH
            )

    @pl.when((z == NZ - 1) & has_down)
    def _():
        pl.semaphore_signal(edge, inc=1, device_id=(row + 1, col), device_id_type=MESH)

    own = [
        send(rbuf.at[col], rbuf.at[col], rsend.at[k], rrecv.at[col], (row, (col + k) % NCOL))
        for k in range(1, NCOL)
    ]
    for copy in own:
        copy.start()

    layout = [(w_out_hbm, w_out)]
    for taps, wide, narrow in ((one_hbm, one_wide, one_narrow), (two_hbm, two_wide, two_narrow)):
        wide[3 * CH :, 0:CH] = jnp.zeros((CH, CH), BF16)
        for p in range(3):
            for q in range(2):
                layout.append((taps.at[3 * p + q], wide.at[p * CH : (p + 1) * CH, q * CH : (q + 1) * CH]))
        layout.append((taps.at[8], wide.at[3 * CH :, CH:]))
        for p in range(2):
            layout.append((taps.at[3 * p + 2], narrow.at[p * CH : (p + 1) * CH]))
    weights = [
        pltpu.make_async_copy(src, dst, weight_sem.at[k]) for k, (src, dst) in enumerate(layout)
    ]
    for copy in weights:
        copy.start()

    def arrived(ref, sem):
        pltpu.make_async_copy(ref, ref, sem).wait()

    for k in range(1, NY):
        at = (y + k) % NY
        arrived(ybuf.at[at], yrecv.at[at])

    @pl.when(takes_left | takes_right)
    def _():
        arrived(ybuf.at[NY], yrecv.at[NY])

    def along(k):
        return send(ybuf, zbuf.at[z], zsend.at[k], zrecv.at[z], (row_at(x, y, k), col))

    for k in range(NZ - 1):
        @pl.when(k < z)
        def _():
            along(k).start()

    zbuf[z] = ybuf[...]
    for k in range(1, NZ):
        @pl.when(k > z)
        def _():
            pl.semaphore_wait(ready.at[k], 1)
            along(k).start()

    loads[4].wait()
    loads[5].wait()
    for k in range(1, NCOL):
        at = (col + k) % NCOL
        arrived(rbuf.at[at], rrecv.at[at])
    sums = jnp.zeros((TR, CH), F32)
    for k in range(NCOL):
        sums = sums + jnp.dot(
            rbuf[k], w_row[k * CH : (k + 1) * CH, :], preferred_element_type=F32
        )
    pbuf[1] = sums.astype(BF16)

    def to_next(block, to_row):
        return [
            send(pbuf.at[1], pbuf.at[block], psend.at[block], precv.at[block], (to_row, col)),
            send(lbuf.at[1], lbuf.at[block], lsend.at[block], lrecv.at[block], (to_row, col)),
        ]

    @pl.when(has_down)
    def _():
        for copy in to_next(0, row + 1):
            copy.start()

    @pl.when(z > 0)
    def _():
        for copy in to_next(2, row - 1):
            copy.start()

    colf[0:8, :] = jnp.zeros((8, CH), F32)
    colf[WIDE - 8 : WIDE, :] = jnp.zeros((8, CH), F32)
    block = NY * NZ
    flat[block + NZ :, :] = jnp.zeros((CHUNK - block - NZ, CH), F32)

    for k in range(1, NZ):
        at = (z + k) % NZ
        arrived(zbuf.at[at], zrecv.at[at])

    for a in range(NY + 1):
        for b in range(NZ):
            flat[a * NZ + b : a * NZ + b + 1, :] = zbuf[b, a]
    xbuf[x] = flat[...].astype(BF16)

    xs = []
    for k in range(1, NX):
        to = (x + k) % NX
        copy = send(xbuf.at[x], xbuf.at[x], xsend.at[k], xrecv.at[x], (row_at(to, y, z), col))
        copy.start()
        xs.append(copy)

    @pl.when((z == 0) & has_up)
    def _():
        pl.semaphore_wait(edge, 1)
        for copy in to_next(2, row - 1):
            copy.start()

    @pl.when(has_up)
    def _():
        arrived(pbuf.at[0], precv.at[0])
        arrived(lbuf.at[0], lrecv.at[0])

    @pl.when(has_down)
    def _():
        arrived(pbuf.at[2], precv.at[2])
        arrived(lbuf.at[2], lrecv.at[2])

    rows_out[...] = pbuf[...].reshape(3 * TR, CH).astype(F32)

    offset = jnp.maximum(jnp.maximum(lbuf[0], lbuf[1]), lbuf[2]).astype(F32)
    spot = lax.broadcasted_iota(jnp.int32, (TAB, CH), 0) + (col * TC - row * TR - 2 - (EXT - 1) + BASE)
    bucket = lax.broadcasted_iota(jnp.int32, (TAB, CH), 1)
    at = spot.astype(F32) + offset[0:1, :]
    low = jnp.where(bucket == 0, -1e9, (STEP * (bucket + 16)).astype(F32))
    high = jnp.where(bucket == CH - 1, 1e9, (STEP * (bucket + 17)).astype(F32))
    chosen = jnp.where((at >= low) & (at < high), 1.0, 0.0).astype(BF16)
    table[...] = jnp.dot(chosen, bias_table[...], preferred_element_type=F32)
    for copy in ys + own:
        copy.wait_send()
    for copy in weights:
        copy.wait()
    for k in range(NZ):
        @pl.when(k != z)
        def _():
            along(k).wait_send()

    @pl.when(gives_right)
    def _():
        for copy in margin_copies(col + 1, NY):
            copy.wait_send()

    @pl.when(gives_left)
    def _():
        for copy in margin_copies(col - 1, 2 * NY):
            copy.wait_send()

    @pl.when(has_up)
    def _():
        for copy in to_next(2, row - 1):
            copy.wait_send()

    @pl.when(has_down)
    def _():
        for copy in to_next(0, row + 1):
            copy.wait_send()

    for k in range(1, NX):
        at = (x + k) % NX
        arrived(xbuf.at[at], xrecv.at[at])
    for k in range(NX):
        part = xbuf[k].astype(F32)
        colf[8 + k * block : 8 + (k + 1) * block, :] = part[0:block]
        if k == 0:
            colf[8 + TC : 8 + TC + SIDE, :] = part[block : block + SIDE]
        if k == NX - 1:
            colf[8 - SIDE : 8, :] = part[block + NZ - SIDE : block + NZ]
    for copy in xs:
        copy.wait_send()


def gather(row_feat, col_feat, ids, w_row, w_col, bias_table, w_out, kernel_one, kernel_two):
    vmem = pl.BlockSpec(memory_space=pltpu.VMEM)
    dma = pltpu.SemaphoreType.DMA
    signal = pltpu.SemaphoreType.REGULAR
    return pl.pallas_call(
        gather_kernel,
        out_shape=(
            pltpu.VMEM((WIDE, CH), F32),
            pltpu.VMEM((3 * TR, CH), F32),
            pltpu.VMEM((TAB, CH), F32),
            pltpu.VMEM((CH, CH), BF16),
            pltpu.VMEM((4 * CH, 2 * CH), BF16),
            pltpu.VMEM((2 * CH, CH), BF16),
            pltpu.VMEM((4 * CH, 2 * CH), BF16),
            pltpu.VMEM((2 * CH, CH), BF16),
        ),
        in_specs=[pl.BlockSpec(memory_space=pl.ANY)] * 9,
        out_specs=(vmem,) * 8,
        scratch_shapes=[
            pltpu.VMEM((1, 1, NCOL * CH), BF16),
            pltpu.VMEM((TR, TC), jnp.int32),
            pltpu.VMEM((NCOL * CH, CH), BF16),
            pltpu.VMEM((NCOL * CH, CH), BF16),
            pltpu.VMEM((CH, CH), BF16),
            pltpu.VMEM((NY + 1, 1, CH), F32),
            pltpu.VMEM((NZ, NY + 1, 1, CH), F32),
            pltpu.VMEM((CHUNK, CH), F32),
            pltpu.VMEM((NX, CHUNK, CH), BF16),
            pltpu.VMEM((NCOL, TR, CH), BF16),
            pltpu.VMEM((3, TR, CH), BF16),
            pltpu.VMEM((3, TR, CH), BF16),
            dma((6,)), dma((19,)),
            dma((3 * NY,)), dma((NY + 1,)),
            dma((NZ,)), dma((NZ,)),
            dma((NX,)), dma((NX,)),
            dma((NCOL,)), dma((NCOL,)),
            dma((3,)), dma((3,)),
            dma((3,)), dma((3,)),
            signal, signal((NZ,)), signal,
        ],
        compiler_params=pltpu.CompilerParams(collective_id=0, has_side_effects=True),
    )(row_feat, col_feat, ids, w_row, w_col, bias_table, w_out, kernel_one, kernel_two)


def gelu(value, half):
    inner = value * (0.7978845608028654 + (0.7978845608028654 * 0.044715) * (value * value))
    return (value * half) * (1.0 + jnp.tanh(inner))


def pair_kernel(
    colf, rows_in, table, w_out, one_wide, one_narrow, two_wide, two_narrow,
    out,
    shifted, moved, act0, act1, pair0, pair1,
):
    row, col, _, _, _ = place()
    left = jnp.where(col > 0, 1.0, 0.0).astype(F32)
    right = jnp.where(col < NCOL - 1, 1.0, 0.0).astype(F32)
    edge = jnp.zeros((GROUP, 8, CH), F32)
    shifted[:, WIDE:, :] = edge
    moved[:, 0:8, :] = edge

    def inside(bin):
        return jnp.where((bin >= 0) & (bin < TR * NROW), 0.5, 0.0).astype(F32)

    def keep(acts, k, at, value, half, gap):
        act = gelu(value, half)
        act = jnp.concatenate([act[0:8] * left, act[8 : WIDE - 8], act[WIDE - 8 :] * right], axis=0)
        shifted[k, 0:WIDE, :] = act
        acts[at, :, 0:CH] = act.astype(BF16)
        acts[at, :, CH:] = shifted[k, gap : gap + WIDE, :].astype(BF16)

    def convolve(acts, base, gap, wide, narrow):
        tops = [acts[pl.ds(base + gap * p, GROUP)].reshape(GROUP * WIDE, 2 * CH) for p in range(3)]
        both = jnp.dot(
            jnp.concatenate([tops[0][:, 0:CH], tops[1][:, 0:CH], tops[2]], axis=1),
            wide[...],
            preferred_element_type=F32,
        )
        last = jnp.dot(
            jnp.concatenate([tops[0][:, CH:], tops[1][:, CH:]], axis=1),
            narrow[...],
            preferred_element_type=F32,
        )
        moved[:, 8:, :] = both[:, 0:CH].reshape(GROUP, WIDE, CH)
        return (both[:, CH:] + last).reshape(GROUP, WIDE, CH)

    def first(step, carry):
        base = step * GROUP
        outer = [
            (rows_in[pl.ds(TR - 6 + base + k, 1), :] * colf[...]).astype(BF16) for k in range(GROUP)
        ]
        mixed = jnp.dot(
            jnp.concatenate(outer, axis=0), w_out[...], preferred_element_type=F32
        ).reshape(GROUP, WIDE, CH)
        for k in range(GROUP):
            value = (mixed[k] + table[pl.ds(EXT - 1 - base - k, WIDE), :]).astype(BF16)
            pair0[base + k] = value
            keep(act0, k, base + k, value.astype(F32), inside(row * TR - 6 + base + k), 2)
        return carry

    lax.fori_loop(0, EXT // GROUP, first, 0)

    def second(step, carry):
        base = step * GROUP
        total = convolve(act0, base, 2, one_wide, one_narrow)
        for k in range(GROUP):
            value = (
                pair0[base + 2 + k].astype(F32) + (total[k] + moved[k, 6 : 6 + WIDE, :])
            ).astype(BF16)
            pair1[base + k] = value
            keep(act1, k, base + k, value.astype(F32), inside(row * TR - 4 + base + k), 4)
        return carry

    lax.fori_loop(0, (TR + 8) // GROUP, second, 0)

    def third(step, carry):
        base = step * GROUP
        total = convolve(act1, base, 4, two_wide, two_narrow)
        for k in range(GROUP):
            value = pair1[base + 4 + k].astype(F32)[8 : 8 + TC]
            out[base + k] = (value + (total[k, 8 : 8 + TC] + moved[k, 12 : 12 + TC, :])).astype(BF16)
        return carry

    lax.fori_loop(0, TR // GROUP, third, 0)


def pairs(*gathered):
    vmem = pl.BlockSpec(memory_space=pltpu.VMEM)
    return pl.pallas_call(
        pair_kernel,
        out_shape=jax.ShapeDtypeStruct((TR, TC, CH), BF16),
        in_specs=[vmem] * 8,
        out_specs=vmem,
        scratch_shapes=[
            pltpu.VMEM((GROUP, WIDE + 8, CH), F32),
            pltpu.VMEM((GROUP, WIDE + 8, CH), F32),
            pltpu.VMEM((EXT, WIDE, 2 * CH), BF16),
            pltpu.VMEM((TR + 8, WIDE, 2 * CH), BF16),
            pltpu.VMEM((EXT, WIDE, CH), BF16),
            pltpu.VMEM((TR + 8, WIDE, CH), BF16),
        ],
        compiler_params=pltpu.CompilerParams(vmem_limit_bytes=48 * 1024 * 1024),
    )(*gathered)


def per_device(
    row_feat, col_feat, bucket_ids, w_row, w_col, w_out, bias_table, kernel_one, kernel_two
):
    gathered = gather(
        row_feat, col_feat, bucket_ids, w_row, w_col, bias_table, w_out, kernel_one, kernel_two
    )
    return pairs(*gathered)


def solution(mesh):
    in_specs = (
        P("rows", "cols"),
        P("cols", "rows", None),
        P("rows", "cols"),
        P(),
        P(),
        P(),
        P(),
        P(),
        P(),
    )
    out_specs = P("rows", "cols", None)
    return jax.shard_map(
        per_device, mesh=mesh, in_specs=in_specs, out_specs=out_specs, check_vma=False
    )
```

```python
import functools

import jax
import jax.numpy as jnp
from jax import lax
from jax.experimental import pallas as pl
from jax.experimental.pallas import tpu as pltpu
from jax.sharding import PartitionSpec as P

MESH = pl.DeviceIdType.MESH
F32 = jnp.float32
BF16 = jnp.bfloat16

NX, NY, NZ = 4, 4, 12
NROW, NCOL = NX * NY * NZ, 4
TR, TC, CH = 16, 192, 128
STEP = 24
GROUP = 4
BASE = 3072
LOW = -240
EXT = 28
WIDE = 208
TAB = 240
CHUNK = 64


def place():
    row, col = lax.axis_index("rows"), lax.axis_index("cols")
    return row, col, row // (NY * NZ), (row // NZ) % NY, row % NZ


def row_at(x, y, z):
    return (x * NY + y) * NZ + z


def send(src, dst, send_sem, recv_sem, device):
    return pltpu.make_async_remote_copy(
        src_ref=src,
        dst_ref=dst,
        send_sem=send_sem,
        recv_sem=recv_sem,
        device_id=device,
        device_id_type=MESH,
    )


SIDE = 6


def gather_kernel(
    row_hbm, col_hbm, ids_hbm, w_row_hbm, w_col_hbm, bias_hbm, w_out_hbm, one_hbm, two_hbm,
    colf, rows_out, table, w_out, one_wide, one_narrow, two_wide, two_narrow,
    col_feat, ids, w_row, w_col, bias_table,
    ybuf, zbuf, flat, xbuf, rbuf, pbuf, lbuf,
    load_sem, weight_sem,
    ysend, yrecv, zsend, zrecv, xsend, xrecv, rsend, rrecv, psend, precv, lsend, lrecv,
    below, ready, edge,
):
    row, col, x, y, z = place()
    has_up, has_down = row > 0, row < NROW - 1
    gives_right = (x == NX - 1) & (y == NY - 1) & (col < NCOL - 1)
    gives_left = (x == 0) & (y == 0) & (col > 0)
    takes_left = (x == NX - 1) & (col > 0)
    takes_right = (x == 0) & (col < NCOL - 1)

    loads = [
        pltpu.make_async_copy(src, dst, load_sem.at[k])
        for k, (src, dst) in enumerate((
            (col_hbm, col_feat), (w_col_hbm, w_col), (row_hbm, rbuf.at[col]), (ids_hbm, ids),
            (w_row_hbm, w_row), (bias_hbm, bias_table),
        ))
    ]
    for copy in loads:
        copy.start()

    ybuf[NY] = jnp.zeros((1, CH), F32)

    @pl.when(jnp.logical_not(has_up))
    def _():
        pbuf[0] = jnp.zeros((TR, CH), BF16)
        lbuf[0] = jnp.full((TR, CH), LOW, BF16)

    @pl.when(jnp.logical_not(has_down))
    def _():
        pbuf[2] = jnp.zeros((TR, CH), BF16)
        lbuf[2] = jnp.full((TR, CH), LOW, BF16)

    barrier = pltpu.get_barrier_semaphore()

    def greet(device):
        pl.semaphore_signal(barrier, inc=1, device_id=device, device_id_type=MESH)

    for k in range(1, NY):
        greet((row_at(x, (y + k) % NY, z), col))
    for k in range(1, NCOL):
        greet((row, (col + k) % NCOL))

    @pl.when(z > 0)
    def _():
        greet((row - 1, col))

    @pl.when(z < NZ - 1)
    def _():
        greet((row + 1, col))

    @pl.when((z == 0) & has_up)
    def _():
        greet((row - 1, col))

    @pl.when(gives_right)
    def _():
        for k in range(NY):
            greet((row_at(x, k, z), col + 1))

    @pl.when(gives_left)
    def _():
        for k in range(NY):
            greet((row_at(x, k, z), col - 1))

    @pl.when(takes_left)
    def _():
        greet((row_at(x, NY - 1, z), col - 1))

    @pl.when(takes_right)
    def _():
        greet((row_at(x, 0, z), col + 1))

    for k in range(1, NX):
        greet((row_at((x + k) % NX, y, z), col))

    def when_add(cond, amount):
        return jnp.where(cond, amount, 0).astype(jnp.int32)

    expected = (
        NY - 1 + NX - 1 + NCOL - 1
        + when_add(z > 0, 1)
        + when_add(z < NZ - 1, 1)
        + when_add((z == NZ - 1) & has_down, 1)
        + when_add(gives_right, NY)
        + when_add(gives_left, NY)
        + when_add(takes_left, 1)
        + when_add(takes_right, 1)
    )

    loads[0].wait()
    loads[1].wait()
    mine = jnp.dot(col_feat[0], w_col[...], preferred_element_type=F32)
    ybuf[y] = mine.astype(BF16).astype(F32)
    loads[2].wait()
    loads[3].wait()
    b = ids[...]
    i = lax.broadcasted_iota(jnp.int32, (TR, TC), 0) + row * TR
    j = lax.broadcasted_iota(jnp.int32, (TR, TC), 1) + col * TC
    forced = jnp.where(b >= 1, STEP * (b + 16) - (j - i) - BASE, LOW).astype(F32)
    least = jnp.max(jnp.max(forced, axis=1, keepdims=True), axis=0, keepdims=True)
    least = jnp.maximum(least, float(LOW))
    lbuf[1] = jnp.broadcast_to(least, (TR, CH)).astype(BF16)

    pl.semaphore_wait(barrier, expected)

    ys = []
    for k in range(1, NY):
        to = (y + k) % NY
        copy = send(ybuf.at[y], ybuf.at[y], ysend.at[k], yrecv.at[y], (row_at(x, to, z), col))
        copy.start()
        ys.append(copy)

    def margin_copies(to_col, sem):
        return [
            send(ybuf.at[y], ybuf.at[NY], ysend.at[sem + k], yrecv.at[NY], (row_at(x, k, z), to_col))
            for k in range(NY)
        ]

    @pl.when(gives_right)
    def _():
        for copy in margin_copies(col + 1, NY):
            copy.start()

    @pl.when(gives_left)
    def _():
        for copy in margin_copies(col - 1, 2 * NY):
            copy.start()

    @pl.when(z > 1)
    def _():
        pl.semaphore_wait(below, 1)

    @pl.when((z > 0) & (z < NZ - 1))
    def _():
        pl.semaphore_signal(below, inc=1, device_id=(row + 1, col), device_id_type=MESH)

    for k in range(NZ - 1):
        @pl.when(k < z)
        def _():
            pl.semaphore_signal(
                ready.at[z], inc=1, device_id=(row_at(x, y, k), col), device_id_type=MESH
            )

    @pl.when((z == NZ - 1) & has_down)
    def _():
        pl.semaphore_signal(edge, inc=1, device_id=(row + 1, col), device_id_type=MESH)

    own = [
        send(rbuf.at[col], rbuf.at[col], rsend.at[k], rrecv.at[col], (row, (col + k) % NCOL))
        for k in range(1, NCOL)
    ]
    for copy in own:
        copy.start()

    layout = [(w_out_hbm, w_out)]
    for taps, wide, narrow in ((one_hbm, one_wide, one_narrow), (two_hbm, two_wide, two_narrow)):
        wide[3 * CH :, 0:CH] = jnp.zeros((CH, CH), BF16)
        for p in range(3):
            for q in range(2):
                layout.append((taps.at[3 * p + q], wide.at[p * CH : (p + 1) * CH, q * CH : (q + 1) * CH]))
        layout.append((taps.at[8], wide.at[3 * CH :, CH:]))
        for p in range(2):
            layout.append((taps.at[3 * p + 2], narrow.at[p * CH : (p + 1) * CH]))
    weights = [
        pltpu.make_async_copy(src, dst, weight_sem.at[k]) for k, (src, dst) in enumerate(layout)
    ]
    for copy in weights:
        copy.start()

    def arrived(ref, sem):
        pltpu.make_async_copy(ref, ref, sem).wait()

    for k in range(1, NY):
        at = (y + k) % NY
        arrived(ybuf.at[at], yrecv.at[at])

    @pl.when(takes_left | takes_right)
    def _():
        arrived(ybuf.at[NY], yrecv.at[NY])

    def along(k):
        return send(ybuf, zbuf.at[z], zsend.at[k], zrecv.at[z], (row_at(x, y, k), col))

    for k in range(NZ - 1):
        @pl.when(k < z)
        def _():
            along(k).start()

    zbuf[z] = ybuf[...]
    for k in range(1, NZ):
        @pl.when(k > z)
        def _():
            pl.semaphore_wait(ready.at[k], 1)
            along(k).start()

    loads[4].wait()
    loads[5].wait()
    for k in range(1, NCOL):
        at = (col + k) % NCOL
        arrived(rbuf.at[at], rrecv.at[at])
    sums = jnp.zeros((TR, CH), F32)
    for k in range(NCOL):
        sums = sums + jnp.dot(
            rbuf[k], w_row[k * CH : (k + 1) * CH, :], preferred_element_type=F32
        )
    pbuf[1] = sums.astype(BF16)

    def to_next(block, to_row):
        return [
            send(pbuf.at[1], pbuf.at[block], psend.at[block], precv.at[block], (to_row, col)),
            send(lbuf.at[1], lbuf.at[block], lsend.at[block], lrecv.at[block], (to_row, col)),
        ]

    @pl.when(has_down)
    def _():
        for copy in to_next(0, row + 1):
            copy.start()

    @pl.when(z > 0)
    def _():
        for copy in to_next(2, row - 1):
            copy.start()

    colf[0:8, :] = jnp.zeros((8, CH), F32)
    colf[WIDE - 8 : WIDE, :] = jnp.zeros((8, CH), F32)
    block = NY * NZ
    flat[block + NZ :, :] = jnp.zeros((CHUNK - block - NZ, CH), F32)

    for k in range(1, NZ):
        at = (z + k) % NZ
        arrived(zbuf.at[at], zrecv.at[at])

    for a in range(NY + 1):
        for b in range(NZ):
            flat[a * NZ + b : a * NZ + b + 1, :] = zbuf[b, a]
    xbuf[x] = flat[...].astype(BF16)

    xs = []
    for k in range(1, NX):
        to = (x + k) % NX
        copy = send(xbuf.at[x], xbuf.at[x], xsend.at[k], xrecv.at[x], (row_at(to, y, z), col))
        copy.start()
        xs.append(copy)

    @pl.when((z == 0) & has_up)
    def _():
        pl.semaphore_wait(edge, 1)
        for copy in to_next(2, row - 1):
            copy.start()

    @pl.when(has_up)
    def _():
        arrived(pbuf.at[0], precv.at[0])
        arrived(lbuf.at[0], lrecv.at[0])

    @pl.when(has_down)
    def _():
        arrived(pbuf.at[2], precv.at[2])
        arrived(lbuf.at[2], lrecv.at[2])

    rows_out[...] = pbuf[...].reshape(3 * TR, CH).astype(F32)

    offset = jnp.maximum(jnp.maximum(lbuf[0], lbuf[1]), lbuf[2]).astype(F32)
    spot = lax.broadcasted_iota(jnp.int32, (TAB, CH), 0) + (col * TC - row * TR - 2 - (EXT - 1) + BASE)
    bucket = lax.broadcasted_iota(jnp.int32, (TAB, CH), 1)
    at = spot.astype(F32) + offset[0:1, :]
    low = jnp.where(bucket == 0, -1e9, (STEP * (bucket + 16)).astype(F32))
    high = jnp.where(bucket == CH - 1, 1e9, (STEP * (bucket + 17)).astype(F32))
    chosen = jnp.where((at >= low) & (at < high), 1.0, 0.0).astype(BF16)
    table[...] = jnp.dot(chosen, bias_table[...], preferred_element_type=F32)
    for copy in ys + own:
        copy.wait_send()
    for copy in weights:
        copy.wait()
    for k in range(NZ):
        @pl.when(k != z)
        def _():
            along(k).wait_send()

    @pl.when(gives_right)
    def _():
        for copy in margin_copies(col + 1, NY):
            copy.wait_send()

    @pl.when(gives_left)
    def _():
        for copy in margin_copies(col - 1, 2 * NY):
            copy.wait_send()

    @pl.when(has_up)
    def _():
        for copy in to_next(2, row - 1):
            copy.wait_send()

    @pl.when(has_down)
    def _():
        for copy in to_next(0, row + 1):
            copy.wait_send()

    for k in range(1, NX):
        at = (x + k) % NX
        arrived(xbuf.at[at], xrecv.at[at])
    for k in range(NX):
        part = xbuf[k].astype(F32)
        colf[8 + k * block : 8 + (k + 1) * block, :] = part[0:block]
        if k == 0:
            colf[8 + TC : 8 + TC + SIDE, :] = part[block : block + SIDE]
        if k == NX - 1:
            colf[8 - SIDE : 8, :] = part[block + NZ - SIDE : block + NZ]
    for copy in xs:
        copy.wait_send()


def gather(row_feat, col_feat, ids, w_row, w_col, bias_table, w_out, kernel_one, kernel_two):
    vmem = pl.BlockSpec(memory_space=pltpu.VMEM)
    dma = pltpu.SemaphoreType.DMA
    signal = pltpu.SemaphoreType.REGULAR
    return pl.pallas_call(
        gather_kernel,
        out_shape=(
            pltpu.VMEM((WIDE, CH), F32),
            pltpu.VMEM((3 * TR, CH), F32),
            pltpu.VMEM((TAB, CH), F32),
            pltpu.VMEM((CH, CH), BF16),
            pltpu.VMEM((4 * CH, 2 * CH), BF16),
            pltpu.VMEM((2 * CH, CH), BF16),
            pltpu.VMEM((4 * CH, 2 * CH), BF16),
            pltpu.VMEM((2 * CH, CH), BF16),
        ),
        in_specs=[pl.BlockSpec(memory_space=pl.ANY)] * 9,
        out_specs=(vmem,) * 8,
        scratch_shapes=[
            pltpu.VMEM((1, 1, NCOL * CH), BF16),
            pltpu.VMEM((TR, TC), jnp.int32),
            pltpu.VMEM((NCOL * CH, CH), BF16),
            pltpu.VMEM((NCOL * CH, CH), BF16),
            pltpu.VMEM((CH, CH), BF16),
            pltpu.VMEM((NY + 1, 1, CH), F32),
            pltpu.VMEM((NZ, NY + 1, 1, CH), F32),
            pltpu.VMEM((CHUNK, CH), F32),
            pltpu.VMEM((NX, CHUNK, CH), BF16),
            pltpu.VMEM((NCOL, TR, CH), BF16),
            pltpu.VMEM((3, TR, CH), BF16),
            pltpu.VMEM((3, TR, CH), BF16),
            dma((6,)), dma((19,)),
            dma((3 * NY,)), dma((NY + 1,)),
            dma((NZ,)), dma((NZ,)),
            dma((NX,)), dma((NX,)),
            dma((NCOL,)), dma((NCOL,)),
            dma((3,)), dma((3,)),
            dma((3,)), dma((3,)),
            signal, signal((NZ,)), signal,
        ],
        compiler_params=pltpu.CompilerParams(collective_id=0, has_side_effects=True),
    )(row_feat, col_feat, ids, w_row, w_col, bias_table, w_out, kernel_one, kernel_two)


def gelu(value, half):
    inner = value * (0.7978845608028654 + (0.7978845608028654 * 0.044715) * (value * value))
    return (value * half) * (1.0 + jnp.tanh(inner))


def pair_kernel(
    colf, rows_in, table, w_out, one_wide, one_narrow, two_wide, two_narrow,
    out,
    shifted, moved, act0, act1, pair0, pair1, done, out_sem,
):
    row, col, _, _, _ = place()
    left = jnp.where(col > 0, 1.0, 0.0).astype(F32)
    right = jnp.where(col < NCOL - 1, 1.0, 0.0).astype(F32)
    edge = jnp.zeros((GROUP, 8, CH), F32)
    shifted[:, WIDE:, :] = edge
    moved[:, 0:8, :] = edge

    def inside(bin):
        return jnp.where((bin >= 0) & (bin < TR * NROW), 0.5, 0.0).astype(F32)

    def keep(acts, k, at, value, half, gap):
        act = gelu(value, half)
        act = jnp.concatenate([act[0:8] * left, act[8 : WIDE - 8], act[WIDE - 8 :] * right], axis=0)
        shifted[k, 0:WIDE, :] = act
        acts[at, :, 0:CH] = act.astype(BF16)
        acts[at, :, CH:] = shifted[k, gap : gap + WIDE, :].astype(BF16)

    def convolve(acts, base, gap, wide, narrow):
        tops = [acts[pl.ds(base + gap * p, GROUP)].reshape(GROUP * WIDE, 2 * CH) for p in range(3)]
        both = jnp.dot(
            jnp.concatenate([tops[0][:, 0:CH], tops[1][:, 0:CH], tops[2]], axis=1),
            wide[...],
            preferred_element_type=F32,
        )
        last = jnp.dot(
            jnp.concatenate([tops[0][:, CH:], tops[1][:, CH:]], axis=1),
            narrow[...],
            preferred_element_type=F32,
        )
        moved[:, 8:, :] = both[:, 0:CH].reshape(GROUP, WIDE, CH)
        return (both[:, CH:] + last).reshape(GROUP, WIDE, CH)

    def first(step, carry):
        base = step * GROUP
        columns = colf[...].astype(BF16)
        outer = [
            rows_in[pl.ds(TR - 6 + base + k, 1), :].astype(BF16) * columns for k in range(GROUP)
        ]
        mixed = jnp.dot(
            jnp.concatenate(outer, axis=0), w_out[...], preferred_element_type=F32
        ).reshape(GROUP, WIDE, CH)
        for k in range(GROUP):
            value = (mixed[k] + table[pl.ds(EXT - 1 - base - k, WIDE), :]).astype(BF16)
            pair0[base + k] = value
            keep(act0, k, base + k, value.astype(F32), inside(row * TR - 6 + base + k), 2)
        return carry

    lax.fori_loop(0, EXT // GROUP, first, 0)

    def second(step, carry):
        base = step * GROUP
        total = convolve(act0, base, 2, one_wide, one_narrow)
        for k in range(GROUP):
            value = (
                pair0[base + 2 + k].astype(F32) + (total[k] + moved[k, 6 : 6 + WIDE, :])
            ).astype(BF16)
            pair1[base + k] = value
            keep(act1, k, base + k, value.astype(F32), inside(row * TR - 4 + base + k), 4)
        return carry

    lax.fori_loop(0, (TR + 8) // GROUP, second, 0)

    def third(step, carry):
        base = step * GROUP
        total = convolve(act1, base, 4, two_wide, two_narrow)
        for k in range(GROUP):
            value = pair1[base + 4 + k].astype(F32)[8 : 8 + TC]
            done[base + k] = (value + (total[k, 8 : 8 + TC] + moved[k, 12 : 12 + TC, :])).astype(BF16)
        leave(step).start()
        return carry

    def leave(step):
        part = pl.ds(step * GROUP, GROUP)
        return pltpu.make_async_copy(done.at[part], out.at[part], out_sem.at[step])

    lax.fori_loop(0, TR // GROUP, third, 0)
    for k in range(TR // GROUP):
        leave(k).wait()


def pairs(*gathered):
    vmem = pl.BlockSpec(memory_space=pltpu.VMEM)
    return pl.pallas_call(
        pair_kernel,
        out_shape=jax.ShapeDtypeStruct((TR, TC, CH), BF16),
        in_specs=[vmem] * 8,
        out_specs=pl.BlockSpec(memory_space=pl.ANY),
        scratch_shapes=[
            pltpu.VMEM((GROUP, WIDE + 8, CH), F32),
            pltpu.VMEM((GROUP, WIDE + 8, CH), F32),
            pltpu.VMEM((EXT, WIDE, 2 * CH), BF16),
            pltpu.VMEM((TR + 8, WIDE, 2 * CH), BF16),
            pltpu.VMEM((EXT, WIDE, CH), BF16),
            pltpu.VMEM((TR + 8, WIDE, CH), BF16),
            pltpu.VMEM((TR, TC, CH), BF16),
            pltpu.SemaphoreType.DMA((TR // GROUP,)),
        ],
        compiler_params=pltpu.CompilerParams(vmem_limit_bytes=48 * 1024 * 1024),
    )(*gathered)


def per_device(
    row_feat, col_feat, bucket_ids, w_row, w_col, w_out, bias_table, kernel_one, kernel_two
):
    gathered = gather(
        row_feat, col_feat, bucket_ids, w_row, w_col, bias_table, w_out, kernel_one, kernel_two
    )
    return pairs(*gathered)


def solution(mesh):
    in_specs = (
        P("rows", "cols"),
        P("cols", "rows", None),
        P("rows", "cols"),
        P(),
        P(),
        P(),
        P(),
        P(),
        P(),
    )
    out_specs = P("rows", "cols", None)
    return jax.shard_map(
        per_device, mesh=mesh, in_specs=in_specs, out_specs=out_specs, check_vma=False
    )
```
